512 devices in a mesh: win: 64 (over y, z), state: 8 (over x, core).
Axes of the slice: x: 4, y: 4, z: 16, core: 2. Of those that a mesh axis runs over, the one named last changes fastest.
Arguments:
- anomalies: float32 [64, 2048, 256], P('win', 'state'), may hold values from -12 to 12
- mean_state: float32 [64, 2048], P('win', 'state'), may hold values from -6 to 6
- obs_rows: int32 [64, 1024], P('win', 'state'), may hold values from 0 to 255
- obs_precision: float32 [64, 1024], P('win', 'state'), may hold values from 0.001953125 to 0.01953125
Outputs:
- updated: float32 [64, 2048, 256], P('win', 'state')
The draws below stay inside these ranges and needn't reach their ends.
Inputs may be any that keep to these rules, and one draw needn't show every extreme that they name: Observation j of window w reads state row (j // 128) * 256 + obs_rows[w, j], a row of the same block of 256 rows.
All inputs are finite; a program needn't handle non-finite values.
Results may differ from the reference program's by a relative error of at most 0.0003.
Values sent between devices are 32-bit elements; how exact they have to be, the bound alone decides.
No kernel may reach another device: no remote copies, remote signals or barrier semaphores. Data moves between devices by JAX's collectives and lax.ppermute only.
A program may use at most 128 MiB of HBM per device.

```python
import math
import jax
import jax.numpy as jnp
from jax import lax

MEMBERS = 256
ROWS_DEV = 256
OBS_DEV = 128
OUTER = 1
NS_STEPS = 3
WINDOWS = 64
ROWS = 2048
OBS = 1024


def draw_anomalies(key, part):
    key_scale, key_noise = jax.random.split(key, 2)
    log_scale = jax.random.uniform(key_scale, (WINDOWS, ROWS, 1), jnp.float32, math.log(0.3), math.log(3.0))
    values = jax.random.normal(key_noise, (WINDOWS, ROWS, MEMBERS), jnp.float32) * jnp.exp(log_scale)
    return jnp.clip(values, -12.0, 12.0).astype(jnp.float32)


def with_ends(values, rng, low, high):
    spot = [jax.random.randint(jax.random.fold_in(rng, axis), (), 0, length) for axis, length in enumerate(values.shape)]
    main_axis = values.shape.index(max(values.shape))
    next_to = spot[:main_axis] + [(spot[main_axis] + 1) % values.shape[main_axis]] + spot[main_axis + 1:]
    return values.at[tuple(spot)].set(low).at[tuple(next_to)].set(high)


def shard_levels(key, extent, cuts, low, high):
    level, own = 1.0, jax.random.fold_in(key, 6)
    for dim, blocks in cuts:
        steps = jnp.exp(jax.random.uniform(jax.random.fold_in(own, dim), (blocks,), jnp.float32, low / len(cuts), high / len(cuts)))
        level = level * jnp.repeat(steps, extent[dim] // blocks).reshape([-1 if axis == dim else 1 for axis in range(len(extent))])
    return level


def bell_draw(own_key, dims, scale, limit, cuts=(), kind=jnp.bfloat16):
    drawn = jax.random.normal(own_key, dims, jnp.float32) * scale
    if len(cuts) > 0:
        drawn = shard_levels(own_key, dims, cuts, -0.22, 0.18) * drawn
    return jnp.clip(drawn, min=-limit, max=limit).astype(kind)


def setup_inputs(seed: int = 0) -> dict:
    splits = jax.random.split(jax.random.key(seed), 5)
    return {
        "anomalies": draw_anomalies(jax.random.fold_in(splits[4], 71), 0),
        "mean_state": bell_draw(splits[1], (WINDOWS, ROWS), 1.0, 6.0, ((0, 64), (1, 8)), jnp.float32),
        "obs_rows": with_ends(jax.random.randint(splits[2], (WINDOWS, OBS), 0, ROWS_DEV), jax.random.fold_in(splits[2], 1), 0, ROWS_DEV - 1).astype(jnp.int32),
        "obs_precision": jnp.clip(jnp.exp(math.log(0.01953125) - 2.3025851 * jax.random.uniform(splits[3], (WINDOWS, OBS), jnp.float32) ** shard_levels(splits[3], (WINDOWS, OBS), ((0, 64), (1, 8)), -0.2, 0.2)), 0.001953125, 0.01953125),
    }


PRECISE = lax.Precision.HIGHEST

def high_dot(left, right):
    return jnp.dot(left, right, precision=PRECISE, preferred_element_type=jnp.float32)

def inverse_root(gram_matrix):
    unit_matrix = jnp.eye(MEMBERS, dtype=jnp.float32)
    system = unit_matrix + gram_matrix
    frob_scale = jnp.sqrt(jnp.sum(system * system))
    root_iter = system / frob_scale
    inverse = unit_matrix
    for ns_index in range(NS_STEPS):
        factor = 1.5 * unit_matrix - 0.5 * high_dot(inverse, root_iter)
        root_iter = high_dot(root_iter, factor)
        inverse = high_dot(factor, inverse)
    return inverse * (MEMBERS / jnp.trace(inverse))

def window_transform(window_args):
    current, mean_row, row_index, precision = window_args
    obs_block = jnp.arange(OBS, dtype=jnp.int32) // OBS_DEV
    state_index = (obs_block * ROWS_DEV + row_index).astype(jnp.int32)
    picked = jnp.take(current, state_index, axis=0)
    predicted = jnp.tanh(jnp.take(mean_row, state_index)[:, None] + picked)
    centred = (predicted - lax.optimization_barrier(jnp.mean(predicted, axis=1, keepdims=True))) * jnp.sqrt(precision)[:, None]
    gram_matrix = high_dot(centred.T, centred) / (MEMBERS - 1)
    return inverse_root(gram_matrix)

def reference(anomalies, mean_state, obs_rows, obs_precision):
    current = anomalies
    unit_matrix = jnp.eye(MEMBERS, dtype=jnp.float32)
    for sweep_index in range(OUTER):
        transforms = lax.map(window_transform, (current, mean_state, obs_rows, obs_precision))

        def link_window(carry, transform):
            product = high_dot(transform, carry)
            return (product, product)
        unused, carried = lax.scan(link_window, unit_matrix, transforms, reverse=True)
        current = lax.map(lambda window_pair: high_dot(window_pair[0], window_pair[1]), (current, carried))
    return current
```

```python
import functools

import jax
import jax.numpy as jnp
from jax import lax
from jax.experimental import pallas as pl
from jax.experimental.pallas import tpu as pltpu
from jax.sharding import Mesh, PartitionSpec as P

F32 = jnp.float32
BF16 = jnp.bfloat16
N = 256
H = 128
PACK = 272
NS_STEPS = 3


def split(a):
    hi = a.astype(BF16)
    lo = (a - hi.astype(F32)).astype(BF16)
    return hi, lo


def mm(a, b):
    dot = functools.partial(jnp.dot, preferred_element_type=F32)
    return dot(a[0], b[0]) + (dot(a[0], b[1]) + dot(a[1], b[0]))


def eye_mask(n):
    i = lax.broadcasted_iota(jnp.int32, (n, n), 0)
    j = lax.broadcasted_iota(jnp.int32, (n, n), 1)
    return i, j


def column(row, n):
    i, j = eye_mask(n)
    return jnp.sum(jnp.where(i == j, row, 0.0), axis=1, keepdims=True)


def pack(m, out, copies):
    i, j = eye_mask(H)
    first, corner = m[:H, :H], m[H:, H:]
    rows = jnp.where(i <= j, first, corner)
    diag = jnp.sum(jnp.where(i == j, corner, 0.0), axis=0, keepdims=True)
    tail = jnp.where(lax.broadcasted_iota(jnp.int32, (PACK - N, H), 0) == 0, diag, 0.0)
    out[:H, :] = rows
    out[H:N, :] = m[:H, H:]
    out[N:, :] = tail


def unpack(p):
    i, j = eye_mask(H)
    rows, cross, diag = p[:H], p[H:N], p[N:N + 1]
    turned = rows.T
    first = jnp.where(i <= j, rows, turned)
    corner = jnp.where(i > j, rows, jnp.where(i < j, turned, diag))
    top = jnp.concatenate([first, cross], axis=1)
    low = jnp.concatenate([cross.T, corner], axis=1)
    return jnp.concatenate([top, low], axis=0)


def gram_kernel(cur_ref, mean_ref, rows_ref, prec_ref, out_ref):
    value = cur_ref[...] + column(mean_ref[...], N)
    state_row = lax.broadcasted_iota(jnp.int32, (N, H), 0)
    chosen = (state_row == rows_ref[...]).astype(F32).T.astype(BF16)
    dot = functools.partial(jnp.dot, preferred_element_type=F32)
    one = value.astype(BF16)
    rest = value - one.astype(F32)
    two = rest.astype(BF16)
    three = (rest - two.astype(F32)).astype(BF16)
    picked = dot(chosen, one) + (dot(chosen, two) + dot(chosen, three))
    predicted = jnp.tanh(picked)
    centred = predicted - jnp.mean(predicted, axis=1, keepdims=True)
    centred = centred * jnp.sqrt(column(prec_ref[...], H))
    gram = mm(split(centred.T), split(centred)) * (1.0 / (N - 1))
    pack(gram, out_ref, 1)


def root_kernel(parts_ref, out_ref, packed):
    total = (parts_ref[0] + parts_ref[1]) + (parts_ref[2] + parts_ref[3])
    i, j = eye_mask(N)
    unit = jnp.where(i == j, 1.0, 0.0)
    system = unpack(total) + unit
    square = jnp.sum(jnp.sum(system * system, axis=0, keepdims=True), axis=1, keepdims=True)
    root = system * (1.0 / jnp.sqrt(square))
    factor = 1.5 * unit - 0.5 * root
    inverse = split(factor)
    root = split(mm(split(root), inverse))
    for step in range(1, NS_STEPS):
        factor = split(1.5 * unit - 0.5 * mm(inverse, root))
        if step + 1 < NS_STEPS:
            root = split(mm(root, factor))
        last = mm(factor, inverse)
        inverse = split(last)
    diag = jnp.where(i == j, last, 0.0)
    trace = jnp.sum(jnp.sum(diag, axis=0, keepdims=True), axis=1, keepdims=True)
    pack(last * (N / trace), packed, 1)
    core = lax.axis_index("core")
    half = packed[pl.ds(pl.multiple_of(core * (PACK // 2), 8), PACK // 2), :]
    for copy in range(4):
        out_ref[copy] = half


def transforms(parts_ref):
    out = []
    for place in range(4):
        out.append(unpack(jnp.concatenate([parts_ref[0, place], parts_ref[1, place]], axis=0)))
    return out


def half_of(total, half_ref):
    core = lax.axis_index("core")

    @pl.when(core == 0)
    def _():
        half_ref[...] = total[:H]

    @pl.when(core == 1)
    def _():
        half_ref[...] = total[H:]


def quad_kernel(parts_ref, total_ref, half_ref):
    one, two, three, four = [split(t) for t in transforms(parts_ref)]
    total = mm(split(mm(one, two)), split(mm(three, four)))
    total_ref[...] = total
    half_of(total, half_ref)


def quad_apply_kernel(parts_ref, cur_ref, out_ref):
    mine = lax.axis_index("zl")
    out_ref[...] = cur_ref[...]
    for place in range(4):

        @pl.when(place >= mine)
        def _():
            t = unpack(jnp.concatenate([parts_ref[0, place], parts_ref[1, place]], axis=0))
            out_ref[...] = mm(split(out_ref[...]), split(t))


def pair_kernel(first_of, copies, mine_ref, other_ref, total_ref, half_ref):
    first = first_of(lax.axis_index("zh"))

    @pl.when(first)
    def _():
        total_ref[...] = mm(split(mine_ref[...]), split(other_ref[...]))

    @pl.when(jnp.logical_not(first))
    def _():
        total_ref[...] = mm(split(other_ref[...]), split(mine_ref[...]))

    core = lax.axis_index("core")
    half = total_ref[pl.ds(pl.multiple_of(core * H, 8), H), :]
    if copies:
        for copy in range(copies):
            half_ref[copy] = half
    else:
        half_ref[...] = half


def pair_apply_kernel(first_of, other_ref, cur_ref, out_ref):
    first = first_of(lax.axis_index("zh"))

    @pl.when(first)
    def _():
        out_ref[...] = mm(split(cur_ref[...]), split(other_ref[...]))

    @pl.when(jnp.logical_not(first))
    def _():
        out_ref[...] = cur_ref[...]


def row_apply_kernel(parts_ref, cur_ref, out_ref):
    mine = lax.axis_index("y")
    out_ref[...] = cur_ref[...]
    for place in range(1, 4):

        @pl.when(place > mine)
        def _():
            t = jnp.concatenate([parts_ref[0, place], parts_ref[1, place]], axis=0)
            out_ref[...] = mm(split(out_ref[...]), split(t))


VMEM = pl.BlockSpec(memory_space=pltpu.VMEM)


def call(kernel, name, outs, args, products, scratch=()):
    many = isinstance(outs, list)
    shapes = [jax.ShapeDtypeStruct(s, F32) for s in (outs if many else [outs])]
    moved = sum(a.size * 4 for a in args) + sum(s.size * 4 for s in shapes)
    return pl.pallas_call(
        kernel,
        name=name,
        out_shape=shapes if many else shapes[0],
        in_specs=[VMEM] * len(args),
        out_specs=[VMEM] * len(shapes) if many else VMEM,
        scratch_shapes=list(scratch),
        cost_estimate=pl.CostEstimate(
            flops=products * 6 * N * N * N, bytes_accessed=moved, transcendentals=0
        ),
    )(*args)


def in_left_quad(quad):
    return quad % 2 == 0


def in_left_half(quad):
    return quad < 2


PAIR_ONE = [(quad, quad ^ 1) for quad in range(4)]
PAIR_TWO = [(quad, quad ^ 3) for quad in range(4)]


def shards(anomalies, mean_state, obs_rows, obs_precision):
    current = anomalies[0]
    gram = call(gram_kernel, "gram", (PACK, H), (current, mean_state, obs_rows, obs_precision), 1)
    both = lax.all_gather(gram, "core")
    spread = jnp.broadcast_to(both[0] + both[1], (4, PACK, H))
    parts = lax.all_to_all(spread, "x", 0, 0)
    half = call(
        root_kernel, "root", (4, PACK // 2, H), (parts,), 6, [pltpu.VMEM((PACK, H), F32)]
    )
    parts = lax.all_gather(lax.all_to_all(half, "zl", 0, 0), "core")
    full = (N, N)
    total, half = call(quad_kernel, "quad", [full, (H, N)], (parts,), 3)
    current = call(quad_apply_kernel, "quad_apply", full, (parts, current), 4)
    for pairs, first_of, copies in ((PAIR_ONE, in_left_quad, 0), (PAIR_TWO, in_left_half, 4)):
        other = lax.ppermute(half, "zh", pairs)
        other = lax.all_gather(other, "core", tiled=True)
        half_shape = (copies, H, N) if copies else (H, N)
        total, half = call(
            functools.partial(pair_kernel, first_of, copies),
            "pair",
            [full, half_shape],
            (total, other),
            1,
        )
        current = call(
            functools.partial(pair_apply_kernel, first_of), "pair_apply", full, (other, current), 1
        )
    parts = lax.all_gather(lax.all_to_all(half, "y", 0, 0), "core")
    return call(row_apply_kernel, "row_apply", full, (parts, current), 3)[None]


def solution(mesh):
    devices = mesh.devices.reshape(4, 4, 4, 4, 2)
    grid = Mesh(devices, ("y", "zh", "zl", "x", "core"))
    win, state = ("y", "zh", "zl"), ("x", "core")
    placed = (P(win, state, None), P(win, state), P(win, state), P(win, state))
    return jax.shard_map(
        shards, mesh=grid, in_specs=placed, out_specs=P(win, state, None), check_vma=False
    )
```

```python
import functools

import jax
import jax.numpy as jnp
from jax import lax
from jax.experimental import pallas as pl
from jax.experimental.pallas import tpu as pltpu
from jax.sharding import Mesh, PartitionSpec as P

F32 = jnp.float32
BF16 = jnp.bfloat16
N = 256
H = 128
PACK = 272
NS_STEPS = 3
VMEM_BYTES = 8 * 1024 * 1024


def split(a):
    hi = a.astype(BF16)
    lo = (a - hi.astype(F32)).astype(BF16)
    return hi, lo


def mm(a, b):
    dot = functools.partial(jnp.dot, preferred_element_type=F32)
    return dot(a[0], b[0]) + (dot(a[0], b[1]) + dot(a[1], b[0]))


def eye_mask(n):
    i = lax.broadcasted_iota(jnp.int32, (n, n), 0)
    j = lax.broadcasted_iota(jnp.int32, (n, n), 1)
    return i, j


def column(row, n):
    i, j = eye_mask(n)
    return jnp.sum(jnp.where(i == j, row, 0.0), axis=1, keepdims=True)


def pack(m, out, copies):
    i, j = eye_mask(H)
    first, corner = m[:H, :H], m[H:, H:]
    rows = jnp.where(i <= j, first, corner)
    diag = jnp.sum(jnp.where(i == j, corner, 0.0), axis=0, keepdims=True)
    tail = jnp.where(lax.broadcasted_iota(jnp.int32, (PACK - N, H), 0) == 0, diag, 0.0)
    out[:H, :] = rows
    out[H:N, :] = m[:H, H:]
    out[N:, :] = tail


def unpack(p):
    i, j = eye_mask(H)
    rows, cross, diag = p[:H], p[H:N], p[N:N + 1]
    turned = rows.T
    first = jnp.where(i <= j, rows, turned)
    corner = jnp.where(i > j, rows, jnp.where(i < j, turned, diag))
    top = jnp.concatenate([first, cross], axis=1)
    low = jnp.concatenate([cross.T, corner], axis=1)
    return jnp.concatenate([top, low], axis=0)


def gram_kernel(cur_ref, mean_ref, rows_ref, prec_ref, out_ref):
    value = cur_ref[...] + column(mean_ref[...], N)
    state_row = lax.broadcasted_iota(jnp.int32, (N, H), 0)
    chosen = (state_row == rows_ref[...]).astype(F32).T.astype(BF16)
    dot = functools.partial(jnp.dot, preferred_element_type=F32)
    one = value.astype(BF16)
    rest = value - one.astype(F32)
    two = rest.astype(BF16)
    three = (rest - two.astype(F32)).astype(BF16)
    picked = dot(chosen, one) + (dot(chosen, two) + dot(chosen, three))
    predicted = jnp.tanh(picked)
    centred = predicted - jnp.mean(predicted, axis=1, keepdims=True)
    centred = centred * jnp.sqrt(column(prec_ref[...], H))
    gram = mm(split(centred.T), split(centred)) * (1.0 / (N - 1))
    pack(gram, out_ref, 1)


def root_kernel(parts_ref, out_ref, packed):
    total = (parts_ref[0] + parts_ref[1]) + (parts_ref[2] + parts_ref[3])
    i, j = eye_mask(N)
    unit = jnp.where(i == j, 1.0, 0.0)
    system = unpack(total) + unit
    square = jnp.sum(jnp.sum(system * system, axis=0, keepdims=True), axis=1, keepdims=True)
    root = system * (1.0 / jnp.sqrt(square))
    factor = 1.5 * unit - 0.5 * root
    inverse = split(factor)
    root = split(mm(split(root), inverse))
    for step in range(1, NS_STEPS):
        factor = split(1.5 * unit - 0.5 * mm(inverse, root))
        if step + 1 < NS_STEPS:
            root = split(mm(root, factor))
        last = mm(factor, inverse)
        inverse = split(last)
    diag = jnp.where(i == j, last, 0.0)
    trace = jnp.sum(jnp.sum(diag, axis=0, keepdims=True), axis=1, keepdims=True)
    pack(last * (N / trace), packed, 1)
    core = lax.axis_index("core")
    half = packed[pl.ds(pl.multiple_of(core * (PACK // 2), 8), PACK // 2), :]
    for copy in range(4):
        out_ref[copy] = half


def transforms(parts_ref):
    out = []
    for place in range(4):
        out.append(unpack(jnp.concatenate([parts_ref[0, place], parts_ref[1, place]], axis=0)))
    return out


def half_of(total, half_ref):
    core = lax.axis_index("core")

    @pl.when(core == 0)
    def _():
        half_ref[...] = total[:H]

    @pl.when(core == 1)
    def _():
        half_ref[...] = total[H:]


def quad_kernel(parts_ref, total_ref, half_ref):
    one, two, three, four = [split(t) for t in transforms(parts_ref)]
    total = mm(split(mm(one, two)), split(mm(three, four)))
    total_ref[...] = total
    half_of(total, half_ref)


def quad_apply_kernel(parts_ref, cur_ref, out_ref):
    mine = lax.axis_index("zl")
    out_ref[...] = cur_ref[...]
    for place in range(4):

        @pl.when(place >= mine)
        def _():
            t = unpack(jnp.concatenate([parts_ref[0, place], parts_ref[1, place]], axis=0))
            out_ref[...] = mm(split(out_ref[...]), split(t))


def pair_kernel(first_of, mine_ref, other_ref, total_ref, half_ref):
    first = first_of(lax.axis_index("zh"))

    @pl.when(first)
    def _():
        total_ref[...] = mm(split(mine_ref[...]), split(other_ref[...]))

    @pl.when(jnp.logical_not(first))
    def _():
        total_ref[...] = mm(split(other_ref[...]), split(mine_ref[...]))

    core = lax.axis_index("core")
    half_ref[...] = total_ref[pl.ds(pl.multiple_of(core * H, 8), H), :]


def pair_apply_kernel(first_of, other_ref, cur_ref, out_ref):
    first = first_of(lax.axis_index("zh"))

    @pl.when(first)
    def _():
        out_ref[...] = mm(split(cur_ref[...]), split(other_ref[...]))

    @pl.when(jnp.logical_not(first))
    def _():
        out_ref[...] = cur_ref[...]


def row_apply_kernel(whole_ref, half_ref, cur_ref, out_ref):
    mine = lax.axis_index("y")
    out_ref[...] = cur_ref[...]

    @pl.when(mine < 3)
    def _():
        out_ref[...] = mm(split(out_ref[...]), split(whole_ref[0]))

    @pl.when(mine < 2)
    def _():
        second = jnp.concatenate([half_ref[0], half_ref[1]], axis=0)
        out_ref[...] = mm(split(out_ref[...]), split(second))

    @pl.when(mine < 1)
    def _():
        out_ref[...] = mm(split(out_ref[...]), split(whole_ref[1]))


VMEM = pl.BlockSpec(memory_space=pltpu.VMEM)


def call(kernel, name, outs, args, products, scratch=()):
    many = isinstance(outs, list)
    shapes = [jax.ShapeDtypeStruct(s, F32) for s in (outs if many else [outs])]
    moved = sum(a.size * 4 for a in args) + sum(s.size * 4 for s in shapes)
    return pl.pallas_call(
        kernel,
        name=name,
        out_shape=shapes if many else shapes[0],
        in_specs=[VMEM] * len(args),
        out_specs=[VMEM] * len(shapes) if many else VMEM,
        scratch_shapes=list(scratch),
        compiler_params=pltpu.CompilerParams(vmem_limit_bytes=VMEM_BYTES),
        cost_estimate=pl.CostEstimate(
            flops=products * 6 * N * N * N, bytes_accessed=moved, transcendentals=0
        ),
    )(*args)


def in_left_quad(quad):
    return quad % 2 == 0


def in_left_half(quad):
    return quad < 2


PAIR_ONE = [(quad, quad ^ 1) for quad in range(4)]
PAIR_TWO = [(quad, quad ^ 3) for quad in range(4)]


def from_later(steps):
    return [
        (2 * row + core, 2 * (row - back) + core)
        for core, back in enumerate(steps)
        for row in range(back, 4)
    ]


ROW_ODD = from_later((1, 3))
ROW_EVEN = from_later((2, 2))


def shards(anomalies, mean_state, obs_rows, obs_precision):
    current = anomalies[0]
    gram = call(gram_kernel, "gram", (PACK, H), (current, mean_state, obs_rows, obs_precision), 1)
    both = lax.all_gather(gram, "core")
    spread = jnp.broadcast_to(both[0] + both[1], (4, PACK, H))
    parts = lax.all_to_all(spread, "x", 0, 0)
    half = call(
        root_kernel, "root", (4, PACK // 2, H), (parts,), 6, [pltpu.VMEM((PACK, H), F32)]
    )
    parts = lax.all_gather(lax.all_to_all(half, "zl", 0, 0), "core")
    full = (N, N)
    total, half = call(quad_kernel, "quad", [full, (H, N)], (parts,), 3)
    current = call(quad_apply_kernel, "quad_apply", full, (parts, current), 4)
    for pairs, first_of in ((PAIR_ONE, in_left_quad), (PAIR_TWO, in_left_half)):
        other = lax.ppermute(half, "zh", pairs)
        other = lax.all_gather(other, "core", tiled=True)
        total, half = call(
            functools.partial(pair_kernel, first_of), "pair", [full, (H, N)], (total, other), 1
        )
        current = call(
            functools.partial(pair_apply_kernel, first_of), "pair_apply", full, (other, current), 1
        )
    whole = lax.all_gather(lax.ppermute(total, ("y", "core"), ROW_ODD), "core")
    half = lax.all_gather(lax.ppermute(half, ("y", "core"), ROW_EVEN), "core")
    return call(row_apply_kernel, "row_apply", full, (whole, half, current), 3)[None]


def solution(mesh):
    devices = mesh.devices.reshape(4, 4, 4, 4, 2)
    grid = Mesh(devices, ("y", "zh", "zl", "x", "core"))
    win, state = ("y", "zh", "zl"), ("x", "core")
    placed = (P(win, state, None), P(win, state), P(win, state), P(win, state))
    return jax.shard_map(
        shards, mesh=grid, in_specs=placed, out_specs=P(win, state, None), check_vma=False
    )
```

```python
import functools

import jax
import jax.numpy as jnp
from jax import lax
from jax.experimental import pallas as pl
from jax.experimental.pallas import tpu as pltpu
from jax.sharding import Mesh, PartitionSpec as P

F32 = jnp.float32
BF16 = jnp.bfloat16
N = 256
H = 128
PACK = 272
NS_STEPS = 3
ALL_VMEM = 67043328
VMEM_BYTES = 8 * 1024 * 1024


def split(a):
    hi = a.astype(BF16)
    lo = (a - hi.astype(F32)).astype(BF16)
    return hi, lo


def mm(a, b):
    dot = functools.partial(jnp.dot, preferred_element_type=F32)
    return dot(a[0], b[0]) + (dot(a[0], b[1]) + dot(a[1], b[0]))


def eye_mask(n):
    i = lax.broadcasted_iota(jnp.int32, (n, n), 0)
    j = lax.broadcasted_iota(jnp.int32, (n, n), 1)
    return i, j


def column(row, n):
    i, j = eye_mask(n)
    return jnp.sum(jnp.where(i == j, row, 0.0), axis=1, keepdims=True)


def pack(m, out, copies):
    i, j = eye_mask(H)
    first, corner = m[:H, :H], m[H:, H:]
    rows = jnp.where(i <= j, first, corner)
    diag = jnp.sum(jnp.where(i == j, corner, 0.0), axis=0, keepdims=True)
    tail = jnp.where(lax.broadcasted_iota(jnp.int32, (PACK - N, H), 0) == 0, diag, 0.0)
    out[:H, :] = rows
    out[H:N, :] = m[:H, H:]
    out[N:, :] = tail


def unpack(p):
    i, j = eye_mask(H)
    rows, cross, diag = p[:H], p[H:N], p[N:N + 1]
    turned = rows.T
    first = jnp.where(i <= j, rows, turned)
    corner = jnp.where(i > j, rows, jnp.where(i < j, turned, diag))
    top = jnp.concatenate([first, cross], axis=1)
    low = jnp.concatenate([cross.T, corner], axis=1)
    return jnp.concatenate([top, low], axis=0)


def gram_kernel(*refs):
    sources, out_ref, held, sems = refs[:4], refs[4], refs[5:9], refs[9]
    copies = [
        pltpu.make_async_copy(source, target, sems.at[place])
        for place, (source, target) in enumerate(zip(sources, held))
    ]
    for copy in copies:
        copy.start()
    for copy in copies:
        copy.wait()
    cur_ref, mean_ref, rows_ref, prec_ref = held
    value = cur_ref[...] + column(mean_ref[...], N)
    state_row = lax.broadcasted_iota(jnp.int32, (N, H), 0)
    chosen = (state_row == rows_ref[...]).astype(F32).T.astype(BF16)
    dot = functools.partial(jnp.dot, preferred_element_type=F32)
    one = value.astype(BF16)
    rest = value - one.astype(F32)
    two = rest.astype(BF16)
    three = (rest - two.astype(F32)).astype(BF16)
    picked = dot(chosen, one) + (dot(chosen, two) + dot(chosen, three))
    predicted = jnp.tanh(picked)
    centred = predicted - jnp.mean(predicted, axis=1, keepdims=True)
    centred = centred * jnp.sqrt(column(prec_ref[...], H))
    gram = mm(split(centred.T), split(centred)) * (1.0 / (N - 1))
    pack(gram, out_ref, 1)


def root_kernel(parts_ref, out_ref, packed):
    total = (parts_ref[0] + parts_ref[1]) + (parts_ref[2] + parts_ref[3])
    i, j = eye_mask(N)
    unit = jnp.where(i == j, 1.0, 0.0)
    system = unpack(total) + unit
    square = jnp.sum(jnp.sum(system * system, axis=0, keepdims=True), axis=1, keepdims=True)
    root = system * (1.0 / jnp.sqrt(square))
    factor = 1.5 * unit - 0.5 * root
    inverse = split(factor)
    root = split(mm(split(root), inverse))
    for step in range(1, NS_STEPS):
        factor = split(1.5 * unit - 0.5 * mm(inverse, root))
        if step + 1 < NS_STEPS:
            root = split(mm(root, factor))
        last = mm(factor, inverse)
        inverse = split(last)
    diag = jnp.where(i == j, last, 0.0)
    trace = jnp.sum(jnp.sum(diag, axis=0, keepdims=True), axis=1, keepdims=True)
    pack(last * (N / trace), packed, 1)
    core = lax.axis_index("core")
    half = packed[pl.ds(pl.multiple_of(core * (PACK // 2), 8), PACK // 2), :]
    for copy in range(4):
        out_ref[copy] = half


def transforms(parts_ref):
    out = []
    for place in range(4):
        out.append(unpack(jnp.concatenate([parts_ref[0, place], parts_ref[1, place]], axis=0)))
    return out


def half_of(total, half_ref):
    core = lax.axis_index("core")

    @pl.when(core == 0)
    def _():
        half_ref[...] = total[:H]

    @pl.when(core == 1)
    def _():
        half_ref[...] = total[H:]


def quad_kernel(parts_ref, total_ref, half_ref):
    one, two, three, four = [split(t) for t in transforms(parts_ref)]
    total = mm(split(mm(one, two)), split(mm(three, four)))
    total_ref[...] = total
    half_of(total, half_ref)


def quad_apply_kernel(parts_ref, cur_ref, out_ref):
    mine = lax.axis_index("zl")
    out_ref[...] = cur_ref[...]
    for place in range(4):

        @pl.when(place >= mine)
        def _():
            t = unpack(jnp.concatenate([parts_ref[0, place], parts_ref[1, place]], axis=0))
            out_ref[...] = mm(split(out_ref[...]), split(t))


def ring_kernel(near_ref, mine_ref, total_ref, half_ref, one, two):
    quad = lax.axis_index("zh")
    mine = split(mine_ref[...])
    after = split(near_ref[0, :N])
    before = split(near_ref[1, :N])
    across = split(jnp.concatenate([near_ref[0, N:], near_ref[1, N:]], axis=0))

    @pl.when(quad % 2 == 0)
    def _():
        one[...] = mm(mine, after)
        two[...] = mm(across, before)

    @pl.when(quad % 2 == 1)
    def _():
        one[...] = mm(before, mine)
        two[...] = mm(after, across)

    @pl.when(quad < 2)
    def _():
        total_ref[...] = mm(split(one[...]), split(two[...]))

    @pl.when(quad >= 2)
    def _():
        total_ref[...] = mm(split(two[...]), split(one[...]))

    core = lax.axis_index("core")
    half_ref[...] = total_ref[pl.ds(pl.multiple_of(core * H, 8), H), :]


def apply_kernel(axis, near_ref, cur_ref, out_ref):
    mine = lax.axis_index(axis)
    out_ref[...] = cur_ref[...]

    @pl.when(mine < 3)
    def _():
        out_ref[...] = mm(split(out_ref[...]), split(near_ref[0, :N]))

    @pl.when(mine < 2)
    def _():
        second = jnp.concatenate([near_ref[0, N:], near_ref[1, N:]], axis=0)
        out_ref[...] = mm(split(out_ref[...]), split(second))

    @pl.when(mine < 1)
    def _():
        out_ref[...] = mm(split(out_ref[...]), split(near_ref[1, :N]))


VMEM = pl.BlockSpec(memory_space=pltpu.VMEM)


def call(kernel, name, outs, args, products, scratch=(), space=VMEM, limit=VMEM_BYTES):
    many = isinstance(outs, list)
    shapes = [jax.ShapeDtypeStruct(s, F32) for s in (outs if many else [outs])]
    moved = sum(a.size * 4 for a in args) + sum(s.size * 4 for s in shapes)
    return pl.pallas_call(
        kernel,
        name=name,
        out_shape=shapes if many else shapes[0],
        in_specs=[space] * len(args),
        out_specs=[VMEM] * len(shapes) if many else VMEM,
        scratch_shapes=list(scratch),
        compiler_params=pltpu.CompilerParams(vmem_limit_bytes=limit),
        cost_estimate=pl.CostEstimate(
            flops=products * 6 * N * N * N, bytes_accessed=moved, transcendentals=0
        ),
    )(*args)


RING = 16
NEAR = [
    (2 * z + core, 2 * ((z + step) % RING) + core)
    for core, step in enumerate((-4, 4))
    for z in range(RING)
]
ACROSS = [(z, (11 - z) if z % 8 < 4 else (19 - z)) for z in range(RING)]


def from_later(steps):
    return [
        (2 * row + core, 2 * (row - back) + core)
        for core, back in enumerate(steps)
        for row in range(back, 4)
    ]


ROW_ODD = from_later((1, 3))
ROW_EVEN = from_later((2, 2))


def shards(anomalies, mean_state, obs_rows, obs_precision):
    current = anomalies[0]
    sources = (current, mean_state, obs_rows, obs_precision)
    gram = call(
        gram_kernel,
        "gram",
        (PACK, H),
        sources,
        1,
        [pltpu.VMEM(a.shape, a.dtype) for a in sources] + [pltpu.SemaphoreType.DMA((4,))],
        pl.BlockSpec(memory_space=pltpu.HBM),
        ALL_VMEM - PACK * H * 4,
    )
    both = lax.all_gather(gram, "core")
    spread = jnp.broadcast_to(both[0] + both[1], (4, PACK, H))
    parts = lax.all_to_all(spread, "x", 0, 0)
    half = call(
        root_kernel, "root", (4, PACK // 2, H), (parts,), 6, [pltpu.VMEM((PACK, H), F32)]
    )
    parts = lax.all_gather(lax.all_to_all(half, "zl", 0, 0), "core")
    full = (N, N)
    total, half = call(quad_kernel, "quad", [full, (H, N)], (parts,), 3)
    current = call(quad_apply_kernel, "quad_apply", full, (parts, current), 4)
    across = lax.ppermute(half, ("zh", "zl"), ACROSS)
    near = lax.ppermute(total, ("zh", "zl", "core"), NEAR)
    near = lax.all_gather(jnp.concatenate([near, across], axis=0), "core")
    square = pltpu.VMEM(full, F32)
    total, half = call(
        ring_kernel, "ring", [full, (H, N)], (near, total), 3, [square, square]
    )
    current = call(
        functools.partial(apply_kernel, "zh"), "ring_apply", full, (near, current), 3
    )
    near = lax.ppermute(total, ("y", "core"), ROW_ODD)
    half = lax.ppermute(half, ("y", "core"), ROW_EVEN)
    near = lax.all_gather(jnp.concatenate([near, half], axis=0), "core")
    return call(functools.partial(apply_kernel, "y"), "row_apply", full, (near, current), 3)[None]


def solution(mesh):
    devices = mesh.devices.reshape(4, 4, 4, 4, 2)
    grid = Mesh(devices, ("y", "zh", "zl", "x", "core"))
    win, state = ("y", "zh", "zl"), ("x", "core")
    placed = (P(win, state, None), P(win, state), P(win, state), P(win, state))
    return jax.shard_map(
        shards, mesh=grid, in_specs=placed, out_specs=P(win, state, None), check_vma=False
    )
```

```python
import functools

import jax
import jax.numpy as jnp
from jax import lax
from jax.experimental import pallas as pl
from jax.experimental.pallas import tpu as pltpu
from jax.sharding import Mesh, PartitionSpec as P


F32 = jnp.float32
BF16 = jnp.bfloat16
N = 256
H = 128
PACK = 272
NS_STEPS = 3
ALL_VMEM = 67043328
VMEM_BYTES = 8 * 1024 * 1024


def split(a):
    hi = a.astype(BF16)
    lo = (a - hi.astype(F32)).astype(BF16)
    return hi, lo


def mm(a, b):
    dot = functools.partial(jnp.dot, preferred_element_type=F32)
    return dot(a[0], b[0]) + (dot(a[0], b[1]) + dot(a[1], b[0]))


def eye_mask(n):
    i = lax.broadcasted_iota(jnp.int32, (n, n), 0)
    j = lax.broadcasted_iota(jnp.int32, (n, n), 1)
    return i, j


def column(row, n):
    i, j = eye_mask(n)
    return jnp.sum(jnp.where(i == j, row, 0.0), axis=1, keepdims=True)


def pack(m, out):
    i, j = eye_mask(H)
    first, corner = m[:H, :H], m[H:, H:]
    rows = jnp.where(i <= j, first, corner)
    diag = jnp.sum(jnp.where(i == j, corner, 0.0), axis=0, keepdims=True)
    tail = jnp.where(lax.broadcasted_iota(jnp.int32, (PACK - N, H), 0) == 0, diag, 0.0)
    out[:H, :] = rows
    out[H:N, :] = m[:H, H:]
    out[N:, :] = tail


def unpack(p):
    i, j = eye_mask(H)
    rows, cross, diag = p[:H], p[H:N], p[N:N + 1]
    turned = rows.T
    first = jnp.where(i <= j, rows, turned)
    corner = jnp.where(i > j, rows, jnp.where(i < j, turned, diag))
    top = jnp.concatenate([first, cross], axis=1)
    low = jnp.concatenate([cross.T, corner], axis=1)
    return jnp.concatenate([top, low], axis=0)


def gram_kernel(*refs):
    sources, out_ref, held, sems = refs[:4], refs[4], refs[5:9], refs[9]
    copies = [
        pltpu.make_async_copy(source, target, sems.at[place])
        for place, (source, target) in enumerate(zip(sources, held))
    ]
    for copy in copies:
        copy.start()
    for copy in copies:
        copy.wait()
    cur_ref, mean_ref, rows_ref, prec_ref = held
    value = cur_ref[...] + column(mean_ref[...], N)
    state_row = lax.broadcasted_iota(jnp.int32, (N, H), 0)
    chosen = (state_row == rows_ref[...]).astype(F32).T.astype(BF16)
    dot = functools.partial(jnp.dot, preferred_element_type=F32)
    one = value.astype(BF16)
    rest = value - one.astype(F32)
    two = rest.astype(BF16)
    three = (rest - two.astype(F32)).astype(BF16)
    picked = dot(chosen, one) + (dot(chosen, two) + dot(chosen, three))
    predicted = jnp.tanh(picked)
    centred = predicted - jnp.mean(predicted, axis=1, keepdims=True)
    centred = centred * jnp.sqrt(column(prec_ref[...], H))
    gram = mm(split(centred.T), split(centred)) * (1.0 / (N - 1))
    pack(gram, out_ref)


def root_kernel(parts_ref, out_ref, packed):
    total = (parts_ref[0] + parts_ref[1]) + (parts_ref[2] + parts_ref[3])
    i, j = eye_mask(N)
    unit = jnp.where(i == j, 1.0, 0.0)
    system = unpack(total) + unit
    square = jnp.sum(jnp.sum(system * system, axis=0, keepdims=True), axis=1, keepdims=True)
    root = system * (1.0 / jnp.sqrt(square))
    factor = 1.5 * unit - 0.5 * root
    inverse = split(factor)
    root = split(mm(split(root), inverse))
    for step in range(1, NS_STEPS):
        factor = split(1.5 * unit - 0.5 * mm(inverse, root))
        if step + 1 < NS_STEPS:
            root = split(mm(root, factor))
        last = mm(factor, inverse)
        inverse = split(last)
    diag = jnp.where(i == j, last, 0.0)
    trace = jnp.sum(jnp.sum(diag, axis=0, keepdims=True), axis=1, keepdims=True)
    pack(last * (N / trace), packed)
    core = lax.axis_index("core")
    half = packed[pl.ds(pl.multiple_of(core * (PACK // 2), 8), PACK // 2), :]
    for copy in range(4):
        out_ref[copy] = half


def transforms(parts_ref):
    out = []
    for place in range(4):
        out.append(unpack(jnp.concatenate([parts_ref[0, place], parts_ref[1, place]], axis=0)))
    return out


def half_of(total, half_ref):
    core = lax.axis_index("core")

    @pl.when(core == 0)
    def _():
        half_ref[...] = total[:H]

    @pl.when(core == 1)
    def _():
        half_ref[...] = total[H:]


def quad_kernel(parts_ref, total_ref, half_ref):
    one, two, three, four = [split(t) for t in transforms(parts_ref)]
    total = mm(split(mm(one, two)), split(mm(three, four)))
    total_ref[...] = total
    half_of(total, half_ref)


def quad_apply_kernel(parts_ref, cur_ref, out_ref):
    mine = lax.axis_index("zl")
    out_ref[...] = cur_ref[...]
    for place in range(4):

        @pl.when(place >= mine)
        def _():
            t = unpack(jnp.concatenate([parts_ref[0, place], parts_ref[1, place]], axis=0))
            out_ref[...] = mm(split(out_ref[...]), split(t))


def beside_kernel(near_ref, mine_ref, out_ref):
    quad = lax.axis_index("zh")
    mine = split(mine_ref[...])

    @pl.when(quad % 2 == 0)
    def _():
        out_ref[...] = mm(mine, split(near_ref[0]))

    @pl.when(quad % 2 == 1)
    def _():
        out_ref[...] = mm(split(near_ref[1]), mine)


def ring_kernel(near_ref, across_ref, beside_ref, total_ref, half_ref, two):
    quad = lax.axis_index("zh")
    across = split(jnp.concatenate([across_ref[0], across_ref[1]], axis=0))
    one = split(beside_ref[...])

    @pl.when(quad % 2 == 0)
    def _():
        two[...] = mm(across, split(near_ref[1]))

    @pl.when(quad % 2 == 1)
    def _():
        two[...] = mm(split(near_ref[0]), across)

    @pl.when(quad < 2)
    def _():
        total_ref[...] = mm(one, split(two[...]))

    @pl.when(quad >= 2)
    def _():
        total_ref[...] = mm(split(two[...]), one)

    core = lax.axis_index("core")
    half_ref[...] = total_ref[pl.ds(pl.multiple_of(core * H, 8), H), :]


def first_kernel(axis, near_ref, cur_ref, out_ref):
    mine = lax.axis_index(axis)

    @pl.when(mine < 3)
    def _():
        out_ref[...] = mm(split(cur_ref[...]), split(near_ref[0]))

    @pl.when(mine == 3)
    def _():
        out_ref[...] = cur_ref[...]


def rest_kernel(axis, near_ref, across_ref, cur_ref, out_ref):
    mine = lax.axis_index(axis)

    @pl.when(mine >= 2)
    def _():
        out_ref[...] = cur_ref[...]

    @pl.when(mine < 2)
    def _():
        second = jnp.concatenate([across_ref[0], across_ref[1]], axis=0)
        out_ref[...] = mm(split(cur_ref[...]), split(second))

    @pl.when(mine < 1)
    def _():
        out_ref[...] = mm(split(out_ref[...]), split(near_ref[1]))


VMEM = pl.BlockSpec(memory_space=pltpu.VMEM)


def call(kernel, outs, args, products, scratch=(), space=VMEM, limit=VMEM_BYTES):
    many = isinstance(outs, list)
    shapes = [jax.ShapeDtypeStruct(s, F32) for s in (outs if many else [outs])]
    moved = sum(a.size * 4 for a in args) + sum(s.size * 4 for s in shapes)
    return pl.pallas_call(
        kernel,
        out_shape=shapes if many else shapes[0],
        in_specs=[space] * len(args),
        out_specs=[VMEM] * len(shapes) if many else VMEM,
        scratch_shapes=list(scratch),
        compiler_params=pltpu.CompilerParams(vmem_limit_bytes=limit),
        cost_estimate=pl.CostEstimate(
            flops=products * 6 * N * N * N, bytes_accessed=moved, transcendentals=0
        ),
    )(*args)


RING = 16
NEAR = [
    (2 * z + core, 2 * ((z + step) % RING) + core)
    for core, step in enumerate((-4, 4))
    for z in range(RING)
]
ACROSS = [(z, (11 - z) if z % 8 < 4 else (19 - z)) for z in range(RING)]


def from_later(steps):
    return [
        (2 * row + core, 2 * (row - back) + core)
        for core, back in enumerate(steps)
        for row in range(back, 4)
    ]


ROW_ODD = from_later((1, 3))
ROW_EVEN = [(row, row - 2) for row in range(2, 4)]


def smoother(anomalies, mean_state, obs_rows, obs_precision):
    current = anomalies[0]
    sources = (current, mean_state, obs_rows, obs_precision)
    gram = call(
        gram_kernel,
        (PACK, H),
        sources,
        1,
        [pltpu.VMEM(a.shape, a.dtype) for a in sources] + [pltpu.SemaphoreType.DMA((4,))],
        pl.BlockSpec(memory_space=pltpu.HBM),
        ALL_VMEM - PACK * H * 4,
    )
    both = lax.all_gather(gram, "core")
    spread = jnp.broadcast_to(both[0] + both[1], (4, PACK, H))
    parts = lax.all_to_all(spread, "x", 0, 0)
    half = call(root_kernel, (4, PACK // 2, H), (parts,), 6, [pltpu.VMEM((PACK, H), F32)])
    parts = lax.all_gather(lax.all_to_all(half, "zl", 0, 0), "core")
    full = (N, N)
    total, half = call(quad_kernel, [full, (H, N)], (parts,), 3)
    current = call(quad_apply_kernel, full, (parts, current), 4)
    near, across = exchange(total, half, ("zh", "zl"), NEAR, ACROSS)
    beside = call(beside_kernel, full, (near, total), 1)
    total, half = call(
        ring_kernel, [full, (H, N)], (near, across, beside), 2, [pltpu.VMEM(full, F32)]
    )
    current = apply(current, near, across, "zh")
    near, across = exchange(total, half, ("y",), ROW_ODD, ROW_EVEN)
    return apply(current, near, across, "y")[None]


def exchange(total, half, axes, near_pairs, across_pairs):
    near = lax.ppermute(total, (*axes, "core"), near_pairs)
    across = lax.ppermute(half, axes, across_pairs)
    near = lax.all_gather(near, "core")
    return near, lax.all_gather(across, "core")


def apply(current, near, across, axis):
    first = functools.partial(first_kernel, axis)
    rest = functools.partial(rest_kernel, axis)
    current = call(first, (N, N), (near, current), 1)
    return call(rest, (N, N), (near, across, current), 2)


def solution(mesh):
    devices = mesh.devices.reshape(4, 4, 4, 4, 2)
    grid = Mesh(devices, ("y", "zh", "zl", "x", "core"))
    win, state = ("y", "zh", "zl"), ("x", "core")
    placed = (P(win, state, None), P(win, state), P(win, state), P(win, state))
    return jax.shard_map(
        smoother, mesh=grid, in_specs=placed, out_specs=P(win, state, None), check_vma=False
    )
```

```python
import functools

import jax
import jax.numpy as jnp
from jax import lax
from jax.experimental import pallas as pl
from jax.experimental.pallas import tpu as pltpu
from jax.sharding import Mesh, PartitionSpec as P


F32 = jnp.float32
BF16 = jnp.bfloat16
N = 256
H = 128
PACK = 272
NS_STEPS = 3
VMEM_BYTES = 8 * 1024 * 1024


def split(a):
    hi = a.astype(BF16)
    lo = (a - hi.astype(F32)).astype(BF16)
    return hi, lo


def mm(a, b):
    dot = functools.partial(jnp.dot, preferred_element_type=F32)
    return dot(a[0], b[0]) + (dot(a[0], b[1]) + dot(a[1], b[0]))


def eye_mask(n):
    i = lax.broadcasted_iota(jnp.int32, (n, n), 0)
    j = lax.broadcasted_iota(jnp.int32, (n, n), 1)
    return i, j


def column(row, n):
    i, j = eye_mask(n)
    return jnp.sum(jnp.where(i == j, row, 0.0), axis=1, keepdims=True)


def pack(m, out):
    i, j = eye_mask(H)
    first, corner = m[:H, :H], m[H:, H:]
    rows = jnp.where(i <= j, first, corner)
    diag = jnp.sum(jnp.where(i == j, corner, 0.0), axis=0, keepdims=True)
    tail = jnp.where(lax.broadcasted_iota(jnp.int32, (PACK - N, H), 0) == 0, diag, 0.0)
    out[:H, :] = rows
    out[H:N, :] = m[:H, H:]
    out[N:, :] = tail


def unpack(p):
    i, j = eye_mask(H)
    rows, cross, diag = p[:H], p[H:N], p[N:N + 1]
    turned = rows.T
    first = jnp.where(i <= j, rows, turned)
    corner = jnp.where(i > j, rows, jnp.where(i < j, turned, diag))
    top = jnp.concatenate([first, cross], axis=1)
    low = jnp.concatenate([cross.T, corner], axis=1)
    return jnp.concatenate([top, low], axis=0)


def gram_kernel(*refs):
    sources, out_ref, held, sems = refs[:4], refs[4], refs[5:9], refs[9]
    copies = [
        pltpu.make_async_copy(source, target, sems.at[place])
        for place, (source, target) in enumerate(zip(sources, held))
    ]
    for copy in copies:
        copy.start()
    for copy in copies:
        copy.wait()
    cur_ref, mean_ref, rows_ref, prec_ref = held
    value = cur_ref[...] + column(mean_ref[...], N)
    state_row = lax.broadcasted_iota(jnp.int32, (N, H), 0)
    chosen = (state_row == rows_ref[...]).astype(F32).T.astype(BF16)
    dot = functools.partial(jnp.dot, preferred_element_type=F32)
    one = value.astype(BF16)
    rest = value - one.astype(F32)
    two = rest.astype(BF16)
    three = (rest - two.astype(F32)).astype(BF16)
    picked = dot(chosen, one) + (dot(chosen, two) + dot(chosen, three))
    predicted = jnp.tanh(picked)
    centred = predicted - jnp.mean(predicted, axis=1, keepdims=True)
    centred = centred * jnp.sqrt(column(prec_ref[...], H))
    gram = mm(split(centred.T), split(centred)) * (1.0 / (N - 1))
    pack(gram, out_ref)


def root_kernel(parts_ref, out_ref, packed):
    total = (parts_ref[0] + parts_ref[1]) + (parts_ref[2] + parts_ref[3])
    i, j = eye_mask(N)
    unit = jnp.where(i == j, 1.0, 0.0)
    system = unpack(total) + unit
    square = jnp.sum(jnp.sum(system * system, axis=0, keepdims=True), axis=1, keepdims=True)
    root = system * (1.0 / jnp.sqrt(square))
    factor = 1.5 * unit - 0.5 * root
    inverse = split(factor)
    root = split(mm(split(root), inverse))
    for step in range(1, NS_STEPS):
        factor = split(1.5 * unit - 0.5 * mm(inverse, root))
        if step + 1 < NS_STEPS:
            root = split(mm(root, factor))
        last = mm(factor, inverse)
        inverse = split(last)
    diag = jnp.where(i == j, last, 0.0)
    trace = jnp.sum(jnp.sum(diag, axis=0, keepdims=True), axis=1, keepdims=True)
    pack(last * (N / trace), packed)
    core = lax.axis_index("core")
    half = packed[pl.ds(pl.multiple_of(core * (PACK // 2), 8), PACK // 2), :]
    for copy in range(4):
        out_ref[copy] = half


def transforms(parts_ref):
    out = []
    for place in range(4):
        out.append(unpack(jnp.concatenate([parts_ref[0, place], parts_ref[1, place]], axis=0)))
    return out


def half_of(total, half_ref):
    core = lax.axis_index("core")

    @pl.when(core == 0)
    def _():
        half_ref[...] = total[:H]

    @pl.when(core == 1)
    def _():
        half_ref[...] = total[H:]


def quad_kernel(parts_ref, total_ref, half_ref):
    one, two, three, four = [split(t) for t in transforms(parts_ref)]
    total = mm(split(mm(one, two)), split(mm(three, four)))
    total_ref[...] = total
    half_of(total, half_ref)


def quad_apply_kernel(parts_ref, cur_ref, out_ref):
    mine = lax.axis_index("zl")
    out_ref[...] = cur_ref[...]
    for place in range(4):

        @pl.when(place >= mine)
        def _():
            t = unpack(jnp.concatenate([parts_ref[0, place], parts_ref[1, place]], axis=0))
            out_ref[...] = mm(split(out_ref[...]), split(t))


def beside_kernel(near_ref, mine_ref, out_ref):
    quad = lax.axis_index("zh")
    mine = split(mine_ref[...])

    @pl.when(quad % 2 == 0)
    def _():
        out_ref[...] = mm(mine, split(near_ref[0]))

    @pl.when(quad % 2 == 1)
    def _():
        out_ref[...] = mm(split(near_ref[1]), mine)


def ring_kernel(near_ref, across_ref, beside_ref, total_ref, half_ref, two):
    quad = lax.axis_index("zh")
    across = split(jnp.concatenate([across_ref[0], across_ref[1]], axis=0))
    one = split(beside_ref[...])

    @pl.when(quad % 2 == 0)
    def _():
        two[...] = mm(across, split(near_ref[1]))

    @pl.when(quad % 2 == 1)
    def _():
        two[...] = mm(split(near_ref[0]), across)

    @pl.when(quad < 2)
    def _():
        total_ref[...] = mm(one, split(two[...]))

    @pl.when(quad >= 2)
    def _():
        total_ref[...] = mm(split(two[...]), one)

    core = lax.axis_index("core")
    half_ref[...] = total_ref[pl.ds(pl.multiple_of(core * H, 8), H), :]


def ring_apply_kernel(near_ref, across_ref, cur_ref, out_ref):
    quad = lax.axis_index("zh")
    out_ref[...] = cur_ref[...]

    @pl.when(quad < 3)
    def _():
        out_ref[...] = mm(split(out_ref[...]), split(near_ref[0]))

    @pl.when(quad < 2)
    def _():
        second = jnp.concatenate([across_ref[0], across_ref[1]], axis=0)
        out_ref[...] = mm(split(out_ref[...]), split(second))

    @pl.when(quad < 1)
    def _():
        out_ref[...] = mm(split(out_ref[...]), split(near_ref[1]))


def row_apply_kernel(near_ref, cur_ref, out_ref):
    row = lax.axis_index("y")
    out_ref[...] = cur_ref[...]

    @pl.when(row < 3)
    def _():
        out_ref[...] = mm(split(out_ref[...]), split(near_ref[0, :N]))

    @pl.when(row < 2)
    def _():
        second = jnp.concatenate([near_ref[0, N:], near_ref[1, N:]], axis=0)
        out_ref[...] = mm(split(out_ref[...]), split(second))

    @pl.when(row < 1)
    def _():
        out_ref[...] = mm(split(out_ref[...]), split(near_ref[1, :N]))


VMEM = pl.BlockSpec(memory_space=pltpu.VMEM)


def call(kernel, outs, args, products, scratch=(), space=VMEM, limit=VMEM_BYTES):
    many = isinstance(outs, list)
    shapes = [jax.ShapeDtypeStruct(s, F32) for s in (outs if many else [outs])]
    moved = sum(a.size * 4 for a in args) + sum(s.size * 4 for s in shapes)
    return pl.pallas_call(
        kernel,
        out_shape=shapes if many else shapes[0],
        in_specs=[space] * len(args),
        out_specs=[VMEM] * len(shapes) if many else VMEM,
        scratch_shapes=list(scratch),
        compiler_params=pltpu.CompilerParams(vmem_limit_bytes=limit),
        cost_estimate=pl.CostEstimate(
            flops=products * 6 * N * N * N, bytes_accessed=moved, transcendentals=0
        ),
    )(*args)


RING = 16
NEAR = [
    (2 * z + core, 2 * ((z + step) % RING) + core)
    for core, step in enumerate((-4, 4))
    for z in range(RING)
]
ACROSS = [(z, (11 - z) if z % 8 < 4 else (19 - z)) for z in range(RING)]


def from_later(steps):
    return [
        (2 * row + core, 2 * (row - back) + core)
        for core, back in enumerate(steps)
        for row in range(back, 4)
    ]


ROW_ODD = from_later((1, 3))
ROW_EVEN = [(row, row - 2) for row in range(2, 4)]


def smoother(anomalies, mean_state, obs_rows, obs_precision):
    current = anomalies[0]
    sources = (current, mean_state, obs_rows, obs_precision)
    gram = call(
        gram_kernel,
        (PACK, H),
        [pltpu.with_memory_space_constraint(a, pltpu.HBM) for a in sources],
        1,
        [pltpu.VMEM(a.shape, a.dtype) for a in sources] + [pltpu.SemaphoreType.DMA((4,))],
        pl.BlockSpec(memory_space=pltpu.HBM),
    )
    both = lax.all_gather(gram, "core")
    spread = jnp.broadcast_to(both[0] + both[1], (4, PACK, H))
    parts = lax.all_to_all(spread, "x", 0, 0)
    half = call(root_kernel, (4, PACK // 2, H), (parts,), 6, [pltpu.VMEM((PACK, H), F32)])
    parts = lax.all_gather(lax.all_to_all(half, "zl", 0, 0), "core")
    full = (N, N)
    total, half = call(quad_kernel, [full, (H, N)], (parts,), 3)
    current = call(quad_apply_kernel, full, (parts, current), 4)
    near = lax.ppermute(total, ("zh", "zl", "core"), NEAR)
    across = lax.ppermute(half, ("zh", "zl"), ACROSS)
    near = lax.all_gather(near, "core")
    across = lax.all_gather(across, "core")
    beside = call(beside_kernel, full, (near, total), 1)
    total, half = call(
        ring_kernel, [full, (H, N)], (near, across, beside), 2, [pltpu.VMEM(full, F32)]
    )
    current = call(ring_apply_kernel, full, (near, across, current), 3)
    near = lax.ppermute(total, ("y", "core"), ROW_ODD)
    across = lax.ppermute(half, "y", ROW_EVEN)
    near = lax.all_gather(jnp.concatenate([near, across], axis=0), "core")
    return call(row_apply_kernel, full, (near, current), 3)[None]


def solution(mesh):
    devices = mesh.devices.reshape(4, 4, 4, 4, 2)
    grid = Mesh(devices, ("y", "zh", "zl", "x", "core"))
    win, state = ("y", "zh", "zl"), ("x", "core")
    placed = (P(win, state, None), P(win, state), P(win, state), P(win, state))
    return jax.shard_map(
        smoother, mesh=grid, in_specs=placed, out_specs=P(win, state, None), check_vma=False
    )
```

```python
import functools

import jax
import jax.numpy as jnp
from jax import lax
from jax.experimental import pallas as pl
from jax.experimental.pallas import tpu as pltpu
from jax.sharding import Mesh, PartitionSpec as P


F32 = jnp.float32
BF16 = jnp.bfloat16
N = 256
H = 128
PACK = 272
NS_STEPS = 3
WIDE, THIN = N // 4, N // 8
VMEM_BYTES = 8 * 1024 * 1024


def split(a):
    hi = a.astype(BF16)
    lo = (a - hi.astype(F32)).astype(BF16)
    return hi, lo


def mm(a, b):
    dot = functools.partial(jnp.dot, preferred_element_type=F32)
    return dot(a[0], b[0]) + (dot(a[0], b[1]) + dot(a[1], b[0]))


def eye_mask(n):
    i = lax.broadcasted_iota(jnp.int32, (n, n), 0)
    j = lax.broadcasted_iota(jnp.int32, (n, n), 1)
    return i, j


def column(row, n):
    i, j = eye_mask(n)
    return jnp.sum(jnp.where(i == j, row, 0.0), axis=1, keepdims=True)


def pack(m, out):
    i, j = eye_mask(H)
    first, corner = m[:H, :H], m[H:, H:]
    rows = jnp.where(i <= j, first, corner)
    diag = jnp.sum(jnp.where(i == j, corner, 0.0), axis=0, keepdims=True)
    tail = jnp.where(lax.broadcasted_iota(jnp.int32, (PACK - N, H), 0) == 0, diag, 0.0)
    out[:H, :] = rows
    out[H:N, :] = m[:H, H:]
    out[N:, :] = tail


def unpack(p):
    i, j = eye_mask(H)
    rows, cross, diag = p[:H], p[H:N], p[N:N + 1]
    turned = rows.T
    first = jnp.where(i <= j, rows, turned)
    corner = jnp.where(i > j, rows, jnp.where(i < j, turned, diag))
    top = jnp.concatenate([first, cross], axis=1)
    low = jnp.concatenate([cross.T, corner], axis=1)
    return jnp.concatenate([top, low], axis=0)


def gram_kernel(*refs):
    sources, out_ref, held, sems = refs[:4], refs[4], refs[5:9], refs[9]
    copies = [
        pltpu.make_async_copy(source, target, sems.at[place])
        for place, (source, target) in enumerate(zip(sources, held))
    ]
    for copy in copies:
        copy.start()
    for copy in copies:
        copy.wait()
    cur_ref, mean_ref, rows_ref, prec_ref = held
    value = cur_ref[...] + column(mean_ref[...], N)
    state_row = lax.broadcasted_iota(jnp.int32, (N, H), 0)
    chosen = (state_row == rows_ref[...]).astype(F32).T.astype(BF16)
    dot = functools.partial(jnp.dot, preferred_element_type=F32)
    one = value.astype(BF16)
    rest = value - one.astype(F32)
    two = rest.astype(BF16)
    three = (rest - two.astype(F32)).astype(BF16)
    picked = dot(chosen, one) + (dot(chosen, two) + dot(chosen, three))
    predicted = jnp.tanh(picked)
    centred = predicted - jnp.mean(predicted, axis=1, keepdims=True)
    centred = centred * jnp.sqrt(column(prec_ref[...], H))
    gram = mm(split(centred.T), split(centred)) * (1.0 / (N - 1))
    pack(gram, out_ref)


def root_kernel(parts_ref, out_ref, packed):
    total = (parts_ref[0] + parts_ref[1]) + (parts_ref[2] + parts_ref[3])
    i, j = eye_mask(N)
    unit = jnp.where(i == j, 1.0, 0.0)
    system = unpack(total) + unit
    square = jnp.sum(jnp.sum(system * system, axis=0, keepdims=True), axis=1, keepdims=True)
    root = system * (1.0 / jnp.sqrt(square))
    factor = 1.5 * unit - 0.5 * root
    inverse = split(factor)
    root = split(mm(split(root), inverse))
    for step in range(1, NS_STEPS):
        factor = split(1.5 * unit - 0.5 * mm(inverse, root))
        if step + 1 < NS_STEPS:
            root = split(mm(root, factor))
        last = mm(factor, inverse)
        inverse = split(last)
    diag = jnp.where(i == j, last, 0.0)
    trace = jnp.sum(jnp.sum(diag, axis=0, keepdims=True), axis=1, keepdims=True)
    pack(last * (N / trace), packed)
    core = lax.axis_index("core")
    half = packed[pl.ds(pl.multiple_of(core * (PACK // 2), 8), PACK // 2), :]
    for copy in range(4):
        out_ref[copy] = half


def transforms(parts_ref):
    out = []
    for place in range(4):
        out.append(unpack(jnp.concatenate([parts_ref[0, place], parts_ref[1, place]], axis=0)))
    return out


def slices(total_ref, wide_ref, thin_ref):
    chip = lax.axis_index("x")
    core = lax.axis_index("core")
    wide_ref[...] = total_ref[pl.ds(pl.multiple_of(chip * WIDE, 8), WIDE), :]
    thin_ref[...] = total_ref[pl.ds(pl.multiple_of(core * H + chip * THIN, 8), THIN), :]


def quad_kernel(parts_ref, total_ref, wide_ref, thin_ref):
    one, two, three, four = [split(t) for t in transforms(parts_ref)]
    total_ref[...] = mm(split(mm(one, two)), split(mm(three, four)))
    slices(total_ref, wide_ref, thin_ref)


def quad_apply_kernel(parts_ref, cur_ref, out_ref):
    mine = lax.axis_index("zl")
    out_ref[...] = cur_ref[...]
    for place in range(4):

        @pl.when(place >= mine)
        def _():
            t = unpack(jnp.concatenate([parts_ref[0, place], parts_ref[1, place]], axis=0))
            out_ref[...] = mm(split(out_ref[...]), split(t))


def joined(ring_ref):
    after = ring_ref[0, :, :WIDE].reshape(N, N)
    before = ring_ref[1, :, :WIDE].reshape(N, N)
    across = [ring_ref[core, :, WIDE:].reshape(H, N) for core in range(2)]
    return after, jnp.concatenate(across, axis=0), before


def ring_kernel(ring_ref, mine_ref, total_ref, half_ref, one, two):
    quad = lax.axis_index("zh")
    mine = split(mine_ref[...])
    after, across, before = [split(m) for m in joined(ring_ref)]

    @pl.when(quad % 2 == 0)
    def _():
        one[...] = mm(mine, after)
        two[...] = mm(across, before)

    @pl.when(quad % 2 == 1)
    def _():
        one[...] = mm(before, mine)
        two[...] = mm(after, across)

    @pl.when(quad < 2)
    def _():
        total_ref[...] = mm(split(one[...]), split(two[...]))

    @pl.when(quad >= 2)
    def _():
        total_ref[...] = mm(split(two[...]), split(one[...]))

    core = lax.axis_index("core")
    half_ref[...] = total_ref[pl.ds(pl.multiple_of(core * H, 8), H), :]


def ring_apply_kernel(ring_ref, cur_ref, out_ref):
    quad = lax.axis_index("zh")
    out_ref[...] = cur_ref[...]
    for place, later in enumerate(joined(ring_ref)):

        @pl.when(quad + place < 3)
        def _():
            out_ref[...] = mm(split(out_ref[...]), split(later))


def row_apply_kernel(near_ref, cur_ref, out_ref):
    row = lax.axis_index("y")
    out_ref[...] = cur_ref[...]

    @pl.when(row < 3)
    def _():
        out_ref[...] = mm(split(out_ref[...]), split(near_ref[0, :N]))

    @pl.when(row < 2)
    def _():
        second = jnp.concatenate([near_ref[0, N:], near_ref[1, N:]], axis=0)
        out_ref[...] = mm(split(out_ref[...]), split(second))

    @pl.when(row < 1)
    def _():
        out_ref[...] = mm(split(out_ref[...]), split(near_ref[1, :N]))


VMEM = pl.BlockSpec(memory_space=pltpu.VMEM)


def call(kernel, outs, args, products, scratch=(), space=VMEM, limit=VMEM_BYTES):
    many = isinstance(outs, list)
    shapes = [jax.ShapeDtypeStruct(s, F32) for s in (outs if many else [outs])]
    moved = sum(a.size * 4 for a in args) + sum(s.size * 4 for s in shapes)
    return pl.pallas_call(
        kernel,
        out_shape=shapes if many else shapes[0],
        in_specs=[space] * len(args),
        out_specs=[VMEM] * len(shapes) if many else VMEM,
        scratch_shapes=list(scratch),
        compiler_params=pltpu.CompilerParams(vmem_limit_bytes=limit),
        cost_estimate=pl.CostEstimate(
            flops=products * 6 * N * N * N, bytes_accessed=moved, transcendentals=0
        ),
    )(*args)


RING = 16
NEAR = [
    (2 * z + core, 2 * ((z + step) % RING) + core)
    for core, step in enumerate((-4, 4))
    for z in range(RING)
]
ACROSS = [(z, (11 - z) if z % 8 < 4 else (19 - z)) for z in range(RING)]


def from_later(steps):
    return [
        (2 * row + core, 2 * (row - back) + core)
        for core, back in enumerate(steps)
        for row in range(back, 4)
    ]


ROW_ODD = from_later((1, 3))
ROW_EVEN = [(row, row - 2) for row in range(2, 4)]


def smoother(anomalies, mean_state, obs_rows, obs_precision):
    current = anomalies[0]
    sources = (current, mean_state, obs_rows, obs_precision)
    gram = call(
        gram_kernel,
        (PACK, H),
        [pltpu.with_memory_space_constraint(a, pltpu.HBM) for a in sources],
        1,
        [pltpu.VMEM(a.shape, a.dtype) for a in sources] + [pltpu.SemaphoreType.DMA((4,))],
        pl.BlockSpec(memory_space=pltpu.HBM),
    )
    both = lax.all_gather(gram, "core")
    spread = jnp.broadcast_to(both[0] + both[1], (4, PACK, H))
    parts = lax.all_to_all(spread, "x", 0, 0)
    half = call(root_kernel, (4, PACK // 2, H), (parts,), 6, [pltpu.VMEM((PACK, H), F32)])
    parts = lax.all_gather(lax.all_to_all(half, "zl", 0, 0), "core")
    full = (N, N)
    wide, thin = (WIDE, N), (THIN, N)
    total, wide, thin = call(quad_kernel, [full, wide, thin], (parts,), 3)
    current = call(quad_apply_kernel, full, (parts, current), 4)
    across = lax.ppermute(thin, ("zh", "zl"), ACROSS)
    near = lax.ppermute(wide, ("zh", "zl", "core"), NEAR)
    piece = jnp.concatenate([near, across], axis=0)
    piece = jnp.broadcast_to(piece, (4, WIDE + THIN, N))
    ring = lax.all_gather(lax.all_to_all(piece, "x", 0, 0), "core")
    square = pltpu.VMEM(full, F32)
    total, half = call(ring_kernel, [full, (H, N)], (ring, total), 3, [square, square])
    current = call(ring_apply_kernel, full, (ring, current), 3)
    near = lax.ppermute(total, ("y", "core"), ROW_ODD)
    across = lax.ppermute(half, "y", ROW_EVEN)
    near = lax.all_gather(jnp.concatenate([near, across], axis=0), "core")
    return call(row_apply_kernel, full, (near, current), 3)[None]


def solution(mesh):
    devices = mesh.devices.reshape(4, 4, 4, 4, 2)
    grid = Mesh(devices, ("y", "zh", "zl", "x", "core"))
    win, state = ("y", "zh", "zl"), ("x", "core")
    placed = (P(win, state, None), P(win, state), P(win, state), P(win, state))
    return jax.shard_map(
        smoother, mesh=grid, in_specs=placed, out_specs=P(win, state, None), check_vma=False
    )
```

```python
import functools

import jax
import jax.numpy as jnp
from jax import lax
from jax.experimental import pallas as pl
from jax.experimental.pallas import tpu as pltpu
from jax.sharding import Mesh, PartitionSpec as P


F32 = jnp.float32
BF16 = jnp.bfloat16
N = 256
H = 128
PACK = 272
NS_STEPS = 3
WIDE, THIN = N // 4, N // 8
VMEM_BYTES = 8 * 1024 * 1024


def split(a):
    hi = a.astype(BF16)
    lo = (a - hi.astype(F32)).astype(BF16)
    return hi, lo


def mm(a, b):
    dot = functools.partial(jnp.dot, preferred_element_type=F32)
    return dot(a[0], b[0]) + (dot(a[0], b[1]) + dot(a[1], b[0]))


def eye_mask(n):
    i = lax.broadcasted_iota(jnp.int32, (n, n), 0)
    j = lax.broadcasted_iota(jnp.int32, (n, n), 1)
    return i, j


def column(row, n):
    i, j = eye_mask(n)
    return jnp.sum(jnp.where(i == j, row, 0.0), axis=1, keepdims=True)


def pack(m, out):
    i, j = eye_mask(H)
    first, corner = m[:H, :H], m[H:, H:]
    rows = jnp.where(i <= j, first, corner)
    diag = jnp.sum(jnp.where(i == j, corner, 0.0), axis=0, keepdims=True)
    tail = jnp.where(lax.broadcasted_iota(jnp.int32, (PACK - N, H), 0) == 0, diag, 0.0)
    out[:H, :] = rows
    out[H:N, :] = m[:H, H:]
    out[N:, :] = tail


def unpack(p):
    i, j = eye_mask(H)
    rows, cross, diag = p[:H], p[H:N], p[N:N + 1]
    turned = rows.T
    first = jnp.where(i <= j, rows, turned)
    corner = jnp.where(i > j, rows, jnp.where(i < j, turned, diag))
    top = jnp.concatenate([first, cross], axis=1)
    low = jnp.concatenate([cross.T, corner], axis=1)
    return jnp.concatenate([top, low], axis=0)


def gram_kernel(*refs):
    sources, out_ref, held, sems = refs[:4], refs[4], refs[5:9], refs[9]
    copies = [
        pltpu.make_async_copy(source, target, sems.at[place])
        for place, (source, target) in enumerate(zip(sources, held))
    ]
    for copy in copies:
        copy.start()
    for copy in copies:
        copy.wait()
    cur_ref, mean_ref, rows_ref, prec_ref = held
    value = cur_ref[...] + column(mean_ref[...], N)
    state_row = lax.broadcasted_iota(jnp.int32, (N, H), 0)
    chosen = (state_row == rows_ref[...]).astype(F32).T.astype(BF16)
    dot = functools.partial(jnp.dot, preferred_element_type=F32)
    one = value.astype(BF16)
    rest = value - one.astype(F32)
    two = rest.astype(BF16)
    three = (rest - two.astype(F32)).astype(BF16)
    picked = dot(chosen, one) + (dot(chosen, two) + dot(chosen, three))
    predicted = jnp.tanh(picked)
    centred = predicted - jnp.mean(predicted, axis=1, keepdims=True)
    centred = centred * jnp.sqrt(column(prec_ref[...], H))
    gram = mm(split(centred.T), split(centred)) * (1.0 / (N - 1))
    pack(gram, out_ref)


def root_kernel(parts_ref, out_ref, packed):
    total = (parts_ref[0] + parts_ref[1]) + (parts_ref[2] + parts_ref[3])
    i, j = eye_mask(N)
    unit = jnp.where(i == j, 1.0, 0.0)
    system = unpack(total) + unit
    square = jnp.sum(jnp.sum(system * system, axis=0, keepdims=True), axis=1, keepdims=True)
    root = system * (1.0 / jnp.sqrt(square))
    factor = 1.5 * unit - 0.5 * root
    inverse = split(factor)
    root = split(mm(split(root), inverse))
    for step in range(1, NS_STEPS):
        factor = split(1.5 * unit - 0.5 * mm(inverse, root))
        if step + 1 < NS_STEPS:
            root = split(mm(root, factor))
        last = mm(factor, inverse)
        inverse = split(last)
    diag = jnp.where(i == j, last, 0.0)
    trace = jnp.sum(jnp.sum(diag, axis=0, keepdims=True), axis=1, keepdims=True)
    pack(last * (N / trace), packed)
    core = lax.axis_index("core")
    half = packed[pl.ds(pl.multiple_of(core * (PACK // 2), 8), PACK // 2), :]
    for copy in range(4):
        out_ref[copy] = half


def transforms(parts_ref):
    out = []
    for place in range(4):
        out.append(unpack(jnp.concatenate([parts_ref[0, place], parts_ref[1, place]], axis=0)))
    return out


def slices(total_ref, wide_ref, thin_ref):
    chip = lax.axis_index("x")
    core = lax.axis_index("core")
    wide_ref[...] = total_ref[pl.ds(pl.multiple_of(chip * WIDE, 8), WIDE), :]
    thin_ref[...] = total_ref[pl.ds(pl.multiple_of(core * H + chip * THIN, 8), THIN), :]


def quad_kernel(parts_ref, total_ref, wide_ref, thin_ref):
    one, two, three, four = [split(t) for t in transforms(parts_ref)]
    total_ref[...] = mm(split(mm(one, two)), split(mm(three, four)))
    slices(total_ref, wide_ref, thin_ref)


def quad_apply_kernel(parts_ref, cur_ref, out_ref):
    mine = lax.axis_index("zl")
    out_ref[...] = cur_ref[...]
    for place in range(4):

        @pl.when(place >= mine)
        def _():
            t = unpack(jnp.concatenate([parts_ref[0, place], parts_ref[1, place]], axis=0))
            out_ref[...] = mm(split(out_ref[...]), split(t))


def joined(ring_ref):
    after = ring_ref[0, :, :WIDE].reshape(N, N)
    before = ring_ref[1, :, :WIDE].reshape(N, N)
    across = [ring_ref[core, :, WIDE:].reshape(H, N) for core in range(2)]
    return after, jnp.concatenate(across, axis=0), before


def ring_kernel(ring_ref, mine_ref, total_ref, half_ref, one, two):
    quad = lax.axis_index("zh")
    mine = split(mine_ref[...])
    after, across, before = [split(m) for m in joined(ring_ref)]

    @pl.when(quad % 2 == 0)
    def _():
        one[...] = mm(mine, after)
        two[...] = mm(across, before)

    @pl.when(quad % 2 == 1)
    def _():
        one[...] = mm(before, mine)
        two[...] = mm(after, across)

    @pl.when(quad < 2)
    def _():
        total_ref[...] = mm(split(one[...]), split(two[...]))

    @pl.when(quad >= 2)
    def _():
        total_ref[...] = mm(split(two[...]), split(one[...]))

    core = lax.axis_index("core")
    half_ref[...] = total_ref[pl.ds(pl.multiple_of(core * H, 8), H), :]


def ring_apply_kernel(ring_ref, cur_ref, out_ref):
    quad = lax.axis_index("zh")
    out_ref[...] = cur_ref[...]
    for place, later in enumerate(joined(ring_ref)):

        @pl.when(quad + place < 3)
        def _():
            out_ref[...] = mm(split(out_ref[...]), split(later))


def row_apply_kernel(near_ref, cur_ref, out_ref):
    row = lax.axis_index("y")
    second = jnp.concatenate([near_ref[0, N:], near_ref[1, N:]], axis=0)

    @pl.when(row == 0)
    def _():
        later = mm(split(second), split(near_ref[1, :N]))
        first = mm(split(cur_ref[...]), split(near_ref[0, :N]))
        out_ref[...] = mm(split(first), split(later))

    @pl.when(row == 1)
    def _():
        first = mm(split(cur_ref[...]), split(near_ref[0, :N]))
        out_ref[...] = mm(split(first), split(second))

    @pl.when(row == 2)
    def _():
        out_ref[...] = mm(split(cur_ref[...]), split(near_ref[0, :N]))

    @pl.when(row == 3)
    def _():
        out_ref[...] = cur_ref[...]


VMEM = pl.BlockSpec(memory_space=pltpu.VMEM)


def call(kernel, outs, args, products, scratch=(), space=VMEM, limit=VMEM_BYTES):
    many = isinstance(outs, list)
    shapes = [jax.ShapeDtypeStruct(s, F32) for s in (outs if many else [outs])]
    moved = sum(a.size * 4 for a in args) + sum(s.size * 4 for s in shapes)
    return pl.pallas_call(
        kernel,
        out_shape=shapes if many else shapes[0],
        in_specs=[space] * len(args),
        out_specs=[VMEM] * len(shapes) if many else VMEM,
        scratch_shapes=list(scratch),
        compiler_params=pltpu.CompilerParams(vmem_limit_bytes=limit),
        cost_estimate=pl.CostEstimate(
            flops=products * 6 * N * N * N, bytes_accessed=moved, transcendentals=0
        ),
    )(*args)


RING = 16
NEAR = [
    (2 * z + core, 2 * ((z + step) % RING) + core)
    for core, step in enumerate((-4, 4))
    for z in range(RING)
]
ACROSS = [(z, (11 - z) if z % 8 < 4 else (19 - z)) for z in range(RING)]


def from_later(steps):
    return [
        (2 * row + core, 2 * (row - back) + core)
        for core, back in enumerate(steps)
        for row in range(back, 4)
    ]


ROW_ODD = from_later((1, 3))
ROW_EVEN = [(row, row - 2) for row in range(2, 4)]


def smoother(anomalies, mean_state, obs_rows, obs_precision):
    current = anomalies[0]
    sources = (current, mean_state, obs_rows, obs_precision)
    gram = call(
        gram_kernel,
        (PACK, H),
        [pltpu.with_memory_space_constraint(a, pltpu.HBM) for a in sources],
        1,
        [pltpu.VMEM(a.shape, a.dtype) for a in sources] + [pltpu.SemaphoreType.DMA((4,))],
        pl.BlockSpec(memory_space=pltpu.HBM),
    )
    both = lax.all_gather(gram, "core")
    spread = jnp.broadcast_to(both[0] + both[1], (4, PACK, H))
    parts = lax.all_to_all(spread, "x", 0, 0)
    half = call(root_kernel, (4, PACK // 2, H), (parts,), 6, [pltpu.VMEM((PACK, H), F32)])
    parts = lax.all_gather(lax.all_to_all(half, "zl", 0, 0), "core")
    full = (N, N)
    wide, thin = (WIDE, N), (THIN, N)
    total, wide, thin = call(quad_kernel, [full, wide, thin], (parts,), 3)
    current = call(quad_apply_kernel, full, (parts, current), 4)
    across = lax.ppermute(thin, ("zh", "zl"), ACROSS)
    near = lax.ppermute(wide, ("zh", "zl", "core"), NEAR)
    piece = jnp.concatenate([near, across], axis=0)
    piece = jnp.broadcast_to(piece, (4, WIDE + THIN, N))
    ring = lax.all_gather(lax.all_to_all(piece, "x", 0, 0), "core")
    square = pltpu.VMEM(full, F32)
    total, half = call(ring_kernel, [full, (H, N)], (ring, total), 3, [square, square])
    current = call(ring_apply_kernel, full, (ring, current), 3)
    near = lax.ppermute(total, ("y", "core"), ROW_ODD)
    across = lax.ppermute(half, "y", ROW_EVEN)
    near = lax.all_gather(jnp.concatenate([near, across], axis=0), "core")
    return call(row_apply_kernel, full, (near, current), 3)[None]


def solution(mesh):
    devices = mesh.devices.reshape(4, 4, 4, 4, 2)
    grid = Mesh(devices, ("y", "zh", "zl", "x", "core"))
    win, state = ("y", "zh", "zl"), ("x", "core")
    placed = (P(win, state, None), P(win, state), P(win, state), P(win, state))
    return jax.shard_map(
        smoother, mesh=grid, in_specs=placed, out_specs=P(win, state, None), check_vma=False
    )
```

```python
import functools

import jax
import jax.numpy as jnp
from jax import lax
from jax.experimental import pallas as pl
from jax.experimental.pallas import tpu as pltpu
from jax.sharding import Mesh, PartitionSpec as P


F32 = jnp.float32
BF16 = jnp.bfloat16
N = 256
H = 128
PACK = 272
NS_STEPS = 3
WIDE, THIN = N // 4, N // 8
VMEM_BYTES = 8 * 1024 * 1024


def split(a):
    hi = a.astype(BF16)
    lo = (a - hi.astype(F32)).astype(BF16)
    return hi, lo


def mm(a, b):
    dot = functools.partial(jnp.dot, preferred_element_type=F32)
    return dot(a[0], b[0]) + (dot(a[0], b[1]) + dot(a[1], b[0]))


def eye_mask(n):
    i = lax.broadcasted_iota(jnp.int32, (n, n), 0)
    j = lax.broadcasted_iota(jnp.int32, (n, n), 1)
    return i, j


def column(row, n):
    i, j = eye_mask(n)
    return jnp.sum(jnp.where(i == j, row, 0.0), axis=1, keepdims=True)


def pack(m, out):
    i, j = eye_mask(H)
    first, corner = m[:H, :H], m[H:, H:]
    rows = jnp.where(i <= j, first, corner)
    diag = jnp.sum(jnp.where(i == j, corner, 0.0), axis=0, keepdims=True)
    tail = jnp.where(lax.broadcasted_iota(jnp.int32, (PACK - N, H), 0) == 0, diag, 0.0)
    out[:H, :] = rows
    out[H:N, :] = m[:H, H:]
    out[N:, :] = tail


def unpack(p):
    i, j = eye_mask(H)
    rows, cross, diag = p[:H], p[H:N], p[N:N + 1]
    turned = rows.T
    first = jnp.where(i <= j, rows, turned)
    corner = jnp.where(i > j, rows, jnp.where(i < j, turned, diag))
    top = jnp.concatenate([first, cross], axis=1)
    low = jnp.concatenate([cross.T, corner], axis=1)
    return jnp.concatenate([top, low], axis=0)


def gram_kernel(*refs):
    sources, out_ref, held, sems = refs[:4], refs[4], refs[5:9], refs[9]
    copies = [
        pltpu.make_async_copy(source, target, sems.at[place])
        for place, (source, target) in enumerate(zip(sources, held))
    ]
    for copy in copies:
        copy.start()
    for copy in copies:
        copy.wait()
    cur_ref, mean_ref, rows_ref, prec_ref = held
    value = cur_ref[...] + column(mean_ref[...], N)
    state_row = lax.broadcasted_iota(jnp.int32, (N, H), 0)
    chosen = (state_row == rows_ref[...]).astype(F32).T.astype(BF16)
    dot = functools.partial(jnp.dot, preferred_element_type=F32)
    one = value.astype(BF16)
    rest = value - one.astype(F32)
    two = rest.astype(BF16)
    three = (rest - two.astype(F32)).astype(BF16)
    picked = dot(chosen, one) + (dot(chosen, two) + dot(chosen, three))
    predicted = jnp.tanh(picked)
    centred = predicted - jnp.mean(predicted, axis=1, keepdims=True)
    centred = centred * jnp.sqrt(column(prec_ref[...], H))
    gram = mm(split(centred.T), split(centred)) * (1.0 / (N - 1))
    pack(gram, out_ref)


def root_kernel(parts_ref, out_ref, packed):
    total = (parts_ref[0] + parts_ref[1]) + (parts_ref[2] + parts_ref[3])
    i, j = eye_mask(N)
    unit = jnp.where(i == j, 1.0, 0.0)
    system = unpack(total) + unit
    square = jnp.sum(jnp.sum(system * system, axis=0, keepdims=True), axis=1, keepdims=True)
    root = system * (1.0 / jnp.sqrt(square))
    factor = 1.5 * unit - 0.5 * root
    inverse = split(factor)
    root = split(mm(split(root), inverse))
    for step in range(1, NS_STEPS):
        factor = split(1.5 * unit - 0.5 * mm(inverse, root))
        if step + 1 < NS_STEPS:
            root = split(mm(root, factor))
        last = mm(factor, inverse)
        inverse = split(last)
    diag = jnp.where(i == j, last, 0.0)
    trace = jnp.sum(jnp.sum(diag, axis=0, keepdims=True), axis=1, keepdims=True)
    pack(last * (N / trace), packed)
    core = lax.axis_index("core")
    half = packed[pl.ds(pl.multiple_of(core * (PACK // 2), 8), PACK // 2), :]
    for copy in range(4):
        out_ref[copy] = half


def transforms(parts_ref):
    out = []
    for place in range(4):
        out.append(unpack(jnp.concatenate([parts_ref[0, place], parts_ref[1, place]], axis=0)))
    return out


def slices(total_ref, wide_ref, thin_ref):
    chip = lax.axis_index("x")
    core = lax.axis_index("core")
    wide_ref[...] = total_ref[pl.ds(pl.multiple_of(chip * WIDE, 8), WIDE), :]
    thin_ref[...] = total_ref[pl.ds(pl.multiple_of(core * H + chip * THIN, 8), THIN), :]


def quad_kernel(parts_ref, total_ref, wide_ref, thin_ref):
    one, two, three, four = [split(t) for t in transforms(parts_ref)]
    total_ref[...] = mm(split(mm(one, two)), split(mm(three, four)))
    slices(total_ref, wide_ref, thin_ref)


def quad_apply_kernel(parts_ref, cur_ref, out_ref):
    mine = lax.axis_index("zl")
    out_ref[...] = cur_ref[...]
    for place in range(4):

        @pl.when(place >= mine)
        def _():
            t = unpack(jnp.concatenate([parts_ref[0, place], parts_ref[1, place]], axis=0))
            out_ref[...] = mm(split(out_ref[...]), split(t))


def joined(ring_ref):
    after = ring_ref[0, :, :WIDE].reshape(N, N)
    before = ring_ref[1, :, :WIDE].reshape(N, N)
    across = [ring_ref[core, :, WIDE:].reshape(H, N) for core in range(2)]
    return after, jnp.concatenate(across, axis=0), before


def ring_kernel(ring_ref, mine_ref, total_ref, half_ref, one, two):
    quad = lax.axis_index("zh")
    mine = split(mine_ref[...])
    after, across, before = [split(m) for m in joined(ring_ref)]

    @pl.when(quad % 2 == 0)
    def _():
        one[...] = mm(mine, after)
        two[...] = mm(across, before)

    @pl.when(quad % 2 == 1)
    def _():
        one[...] = mm(before, mine)
        two[...] = mm(after, across)

    @pl.when(quad < 2)
    def _():
        total_ref[...] = mm(split(one[...]), split(two[...]))

    @pl.when(quad >= 2)
    def _():
        total_ref[...] = mm(split(two[...]), split(one[...]))

    core = lax.axis_index("core")
    half_ref[...] = total_ref[pl.ds(pl.multiple_of(core * H, 8), H), :]


def ring_apply_kernel(ring_ref, cur_ref, out_ref):
    quad = lax.axis_index("zh")
    out_ref[...] = cur_ref[...]
    for place, later in enumerate(joined(ring_ref)):

        @pl.when(quad + place < 3)
        def _():
            out_ref[...] = mm(split(out_ref[...]), split(later))


def row_apply_kernel(near_ref, cur_ref, out_ref):
    row = lax.axis_index("y")

    @pl.when(row == 0)
    def _():
        third = jnp.concatenate([near_ref[0, N:], near_ref[1, N:]], axis=0)
        later = mm(split(near_ref[1, :N]), split(third))
        first = mm(split(cur_ref[...]), split(near_ref[0, :N]))
        out_ref[...] = mm(split(first), split(later))

    @pl.when(row == 1)
    def _():
        first = mm(split(cur_ref[...]), split(near_ref[0, :N]))
        out_ref[...] = mm(split(first), split(near_ref[1, :N]))

    @pl.when(row == 2)
    def _():
        out_ref[...] = mm(split(cur_ref[...]), split(near_ref[0, :N]))

    @pl.when(row == 3)
    def _():
        out_ref[...] = cur_ref[...]


VMEM = pl.BlockSpec(memory_space=pltpu.VMEM)


def call(kernel, outs, args, products, scratch=(), space=VMEM, limit=VMEM_BYTES):
    many = isinstance(outs, list)
    shapes = [jax.ShapeDtypeStruct(s, F32) for s in (outs if many else [outs])]
    moved = sum(a.size * 4 for a in args) + sum(s.size * 4 for s in shapes)
    return pl.pallas_call(
        kernel,
        out_shape=shapes if many else shapes[0],
        in_specs=[space] * len(args),
        out_specs=[VMEM] * len(shapes) if many else VMEM,
        scratch_shapes=list(scratch),
        compiler_params=pltpu.CompilerParams(vmem_limit_bytes=limit),
        cost_estimate=pl.CostEstimate(
            flops=products * 6 * N * N * N, bytes_accessed=moved, transcendentals=0
        ),
    )(*args)


RING = 16
NEAR = [
    (2 * z + core, 2 * ((z + step) % RING) + core)
    for core, step in enumerate((-4, 4))
    for z in range(RING)
]
ACROSS = [(z, (11 - z) if z % 8 < 4 else (19 - z)) for z in range(RING)]


def from_later(steps):
    return [
        (2 * row + core, 2 * (row - back) + core)
        for core, back in enumerate(steps)
        for row in range(back, 4)
    ]


ROW_NEAR = from_later((1, 2))
ROW_LAST = [(3, 0)]


def smoother(anomalies, mean_state, obs_rows, obs_precision):
    current = anomalies[0]
    sources = (current, mean_state, obs_rows, obs_precision)
    gram = call(
        gram_kernel,
        (PACK, H),
        [pltpu.with_memory_space_constraint(a, pltpu.HBM) for a in sources],
        1,
        [pltpu.VMEM(a.shape, a.dtype) for a in sources] + [pltpu.SemaphoreType.DMA((4,))],
        pl.BlockSpec(memory_space=pltpu.HBM),
    )
    both = lax.all_gather(gram, "core")
    spread = jnp.broadcast_to(both[0] + both[1], (4, PACK, H))
    parts = lax.all_to_all(spread, "x", 0, 0)
    half = call(root_kernel, (4, PACK // 2, H), (parts,), 6, [pltpu.VMEM((PACK, H), F32)])
    parts = lax.all_gather(lax.all_to_all(half, "zl", 0, 0), "core")
    full = (N, N)
    wide, thin = (WIDE, N), (THIN, N)
    total, wide, thin = call(quad_kernel, [full, wide, thin], (parts,), 3)
    current = call(quad_apply_kernel, full, (parts, current), 4)
    across = lax.ppermute(thin, ("zh", "zl"), ACROSS)
    near = lax.ppermute(wide, ("zh", "zl", "core"), NEAR)
    piece = jnp.concatenate([near, across], axis=0)
    piece = jnp.broadcast_to(piece, (4, WIDE + THIN, N))
    ring = lax.all_gather(lax.all_to_all(piece, "x", 0, 0), "core")
    square = pltpu.VMEM(full, F32)
    total, half = call(ring_kernel, [full, (H, N)], (ring, total), 3, [square, square])
    current = call(ring_apply_kernel, full, (ring, current), 3)
    near = lax.ppermute(total, ("y", "core"), ROW_NEAR)
    across = lax.ppermute(half, "y", ROW_LAST)
    near = lax.all_gather(jnp.concatenate([near, across], axis=0), "core")
    return call(row_apply_kernel, full, (near, current), 3)[None]


def solution(mesh):
    devices = mesh.devices.reshape(4, 4, 4, 4, 2)
    grid = Mesh(devices, ("y", "zh", "zl", "x", "core"))
    win, state = ("y", "zh", "zl"), ("x", "core")
    placed = (P(win, state, None), P(win, state), P(win, state), P(win, state))
    return jax.shard_map(
        smoother, mesh=grid, in_specs=placed, out_specs=P(win, state, None), check_vma=False
    )
```

```python
import functools

import jax
import jax.numpy as jnp
from jax import lax
from jax.experimental import pallas as pl
from jax.experimental.pallas import tpu as pltpu
from jax.sharding import Mesh, PartitionSpec as P


F32 = jnp.float32
BF16 = jnp.bfloat16
N = 256
H = 128
PACK = 272
NS_STEPS = 3
THIN = N // 8
VMEM_BYTES = 8 * 1024 * 1024


def split(a):
    hi = a.astype(BF16)
    lo = (a - hi.astype(F32)).astype(BF16)
    return hi, lo


def mm(a, b):
    dot = functools.partial(jnp.dot, preferred_element_type=F32)
    return dot(a[0], b[0]) + (dot(a[0], b[1]) + dot(a[1], b[0]))


def eye_mask(n):
    i = lax.broadcasted_iota(jnp.int32, (n, n), 0)
    j = lax.broadcasted_iota(jnp.int32, (n, n), 1)
    return i, j


def column(row, n):
    i, j = eye_mask(n)
    return jnp.sum(jnp.where(i == j, row, 0.0), axis=1, keepdims=True)


def pack(m, out):
    i, j = eye_mask(H)
    first, corner = m[:H, :H], m[H:, H:]
    rows = jnp.where(i <= j, first, corner)
    diag = jnp.sum(jnp.where(i == j, corner, 0.0), axis=0, keepdims=True)
    tail = jnp.where(lax.broadcasted_iota(jnp.int32, (PACK - N, H), 0) == 0, diag, 0.0)
    out[:H, :] = rows
    out[H:N, :] = m[:H, H:]
    out[N:, :] = tail


def unpack(p):
    i, j = eye_mask(H)
    rows, cross, diag = p[:H], p[H:N], p[N:N + 1]
    turned = rows.T
    first = jnp.where(i <= j, rows, turned)
    corner = jnp.where(i > j, rows, jnp.where(i < j, turned, diag))
    top = jnp.concatenate([first, cross], axis=1)
    low = jnp.concatenate([cross.T, corner], axis=1)
    return jnp.concatenate([top, low], axis=0)


def gram_kernel(*refs):
    sources, out_ref, held, sems = refs[:4], refs[4], refs[5:9], refs[9]
    copies = [
        pltpu.make_async_copy(source, target, sems.at[place])
        for place, (source, target) in enumerate(zip(sources, held))
    ]
    for copy in copies:
        copy.start()
    for copy in copies:
        copy.wait()
    cur_ref, mean_ref, rows_ref, prec_ref = held
    value = cur_ref[...] + column(mean_ref[...], N)
    state_row = lax.broadcasted_iota(jnp.int32, (N, H), 0)
    chosen = (state_row == rows_ref[...]).astype(F32).T.astype(BF16)
    dot = functools.partial(jnp.dot, preferred_element_type=F32)
    one = value.astype(BF16)
    rest = value - one.astype(F32)
    two = rest.astype(BF16)
    three = (rest - two.astype(F32)).astype(BF16)
    picked = dot(chosen, one) + (dot(chosen, two) + dot(chosen, three))
    predicted = jnp.tanh(picked)
    centred = predicted - jnp.mean(predicted, axis=1, keepdims=True)
    centred = centred * jnp.sqrt(column(prec_ref[...], H))
    gram = mm(split(centred.T), split(centred)) * (1.0 / (N - 1))
    pack(gram, out_ref)


def root_kernel(parts_ref, out_ref, packed):
    total = (parts_ref[0] + parts_ref[1]) + (parts_ref[2] + parts_ref[3])
    i, j = eye_mask(N)
    unit = jnp.where(i == j, 1.0, 0.0)
    system = unpack(total) + unit
    square = jnp.sum(jnp.sum(system * system, axis=0, keepdims=True), axis=1, keepdims=True)
    root = system * (1.0 / jnp.sqrt(square))
    factor = 1.5 * unit - 0.5 * root
    inverse = split(factor)
    root = split(mm(split(root), inverse))
    for step in range(1, NS_STEPS):
        factor = split(1.5 * unit - 0.5 * mm(inverse, root))
        if step + 1 < NS_STEPS:
            root = split(mm(root, factor))
        last = mm(factor, inverse)
        inverse = split(last)
    diag = jnp.where(i == j, last, 0.0)
    trace = jnp.sum(jnp.sum(diag, axis=0, keepdims=True), axis=1, keepdims=True)
    pack(last * (N / trace), packed)
    core = lax.axis_index("core")
    half = packed[pl.ds(pl.multiple_of(core * (PACK // 2), 8), PACK // 2), :]
    for copy in range(4):
        out_ref[copy] = half


def transforms(parts_ref):
    out = []
    for place in range(4):
        out.append(unpack(jnp.concatenate([parts_ref[0, place], parts_ref[1, place]], axis=0)))
    return out


def quad_kernel(parts_ref, total_ref, slice_ref):
    one, two, three, four = [split(t) for t in transforms(parts_ref)]
    total_ref[...] = mm(split(mm(one, two)), split(mm(three, four)))
    place = 2 * lax.axis_index("x") + lax.axis_index("core")
    rows = total_ref[pl.ds(pl.multiple_of(place * THIN, 8), THIN), :]
    for copy in range(4):
        slice_ref[copy] = rows


def pick_kernel(slices_ref, out_ref):
    quad = lax.axis_index("zh")
    for place in range(3):
        rows = slices_ref[lax.rem(quad + place + 1, 4)]
        for copy in range(4):
            out_ref[copy, place * THIN : (place + 1) * THIN, :] = rows


def quad_apply_kernel(parts_ref, cur_ref, out_ref):
    mine = lax.axis_index("zl")
    out_ref[...] = cur_ref[...]
    for place in range(4):

        @pl.when(place >= mine)
        def _():
            t = unpack(jnp.concatenate([parts_ref[0, place], parts_ref[1, place]], axis=0))
            out_ref[...] = mm(split(out_ref[...]), split(t))


def joined(ring_ref):
    out = []
    for place in range(3):
        rows = slice(place * THIN, (place + 1) * THIN)
        pieces = [ring_ref[core, chip, rows] for chip in range(4) for core in range(2)]
        out.append(jnp.concatenate(pieces, axis=0))
    return out


def ring_kernel(ring_ref, mine_ref, total_ref, half_ref, one, two):
    quad = lax.axis_index("zh")
    mine = split(mine_ref[...])
    after, across, before = [split(m) for m in joined(ring_ref)]

    @pl.when(quad % 2 == 0)
    def _():
        one[...] = mm(mine, after)
        two[...] = mm(across, before)

    @pl.when(quad % 2 == 1)
    def _():
        one[...] = mm(before, mine)
        two[...] = mm(after, across)

    @pl.when(quad < 2)
    def _():
        total_ref[...] = mm(split(one[...]), split(two[...]))

    @pl.when(quad >= 2)
    def _():
        total_ref[...] = mm(split(two[...]), split(one[...]))

    core = lax.axis_index("core")
    half_ref[...] = total_ref[pl.ds(pl.multiple_of(core * H, 8), H), :]


def ring_apply_kernel(ring_ref, cur_ref, out_ref):
    quad = lax.axis_index("zh")
    out_ref[...] = cur_ref[...]
    for place, later in enumerate(joined(ring_ref)):

        @pl.when(quad + place < 3)
        def _():
            out_ref[...] = mm(split(out_ref[...]), split(later))


def row_apply_kernel(near_ref, cur_ref, out_ref):
    row = lax.axis_index("y")

    @pl.when(row == 0)
    def _():
        third = jnp.concatenate([near_ref[0, N:], near_ref[1, N:]], axis=0)
        later = mm(split(near_ref[1, :N]), split(third))
        first = mm(split(cur_ref[...]), split(near_ref[0, :N]))
        out_ref[...] = mm(split(first), split(later))

    @pl.when(row == 1)
    def _():
        first = mm(split(cur_ref[...]), split(near_ref[0, :N]))
        out_ref[...] = mm(split(first), split(near_ref[1, :N]))

    @pl.when(row == 2)
    def _():
        out_ref[...] = mm(split(cur_ref[...]), split(near_ref[0, :N]))

    @pl.when(row == 3)
    def _():
        out_ref[...] = cur_ref[...]


VMEM = pl.BlockSpec(memory_space=pltpu.VMEM)


def call(kernel, outs, args, products, scratch=(), space=VMEM, limit=VMEM_BYTES):
    many = isinstance(outs, list)
    shapes = [jax.ShapeDtypeStruct(s, F32) for s in (outs if many else [outs])]
    moved = sum(a.size * 4 for a in args) + sum(s.size * 4 for s in shapes)
    return pl.pallas_call(
        kernel,
        out_shape=shapes if many else shapes[0],
        in_specs=[space] * len(args),
        out_specs=[VMEM] * len(shapes) if many else VMEM,
        scratch_shapes=list(scratch),
        compiler_params=pltpu.CompilerParams(vmem_limit_bytes=limit),
        cost_estimate=pl.CostEstimate(
            flops=products * 6 * N * N * N, bytes_accessed=moved, transcendentals=0
        ),
    )(*args)


def from_later(steps):
    return [
        (2 * row + core, 2 * (row - back) + core)
        for core, back in enumerate(steps)
        for row in range(back, 4)
    ]


ROW_NEAR = from_later((1, 2))
ROW_LAST = [(3, 0)]


def smoother(anomalies, mean_state, obs_rows, obs_precision):
    current = anomalies[0]
    sources = (current, mean_state, obs_rows, obs_precision)
    gram = call(
        gram_kernel,
        (PACK, H),
        [pltpu.with_memory_space_constraint(a, pltpu.HBM) for a in sources],
        1,
        [pltpu.VMEM(a.shape, a.dtype) for a in sources] + [pltpu.SemaphoreType.DMA((4,))],
        pl.BlockSpec(memory_space=pltpu.HBM),
    )
    both = lax.all_gather(gram, "core")
    spread = jnp.broadcast_to(both[0] + both[1], (4, PACK, H))
    parts = lax.all_to_all(spread, "x", 0, 0)
    half = call(root_kernel, (4, PACK // 2, H), (parts,), 6, [pltpu.VMEM((PACK, H), F32)])
    parts = lax.all_gather(lax.all_to_all(half, "zl", 0, 0), "core")
    full = (N, N)
    total, piece = call(quad_kernel, [full, (4, THIN, N)], (parts,), 3)
    current = call(quad_apply_kernel, full, (parts, current), 4)
    piece = lax.all_to_all(piece, "zh", 0, 0)
    piece = call(pick_kernel, (4, 3 * THIN, N), (piece,), 0)
    ring = lax.all_gather(lax.all_to_all(piece, "x", 0, 0), "core")
    square = pltpu.VMEM(full, F32)
    total, half = call(ring_kernel, [full, (H, N)], (ring, total), 3, [square, square])
    current = call(ring_apply_kernel, full, (ring, current), 3)
    near = lax.ppermute(total, ("y", "core"), ROW_NEAR)
    across = lax.ppermute(half, "y", ROW_LAST)
    near = lax.all_gather(jnp.concatenate([near, across], axis=0), "core")
    return call(row_apply_kernel, full, (near, current), 3)[None]


def solution(mesh):
    devices = mesh.devices.reshape(4, 4, 4, 4, 2)
    grid = Mesh(devices, ("y", "zh", "zl", "x", "core"))
    win, state = ("y", "zh", "zl"), ("x", "core")
    placed = (P(win, state, None), P(win, state), P(win, state), P(win, state))
    return jax.shard_map(
        smoother, mesh=grid, in_specs=placed, out_specs=P(win, state, None), check_vma=False
    )
```

```python
import functools

import jax
import jax.numpy as jnp
from jax import lax
from jax.experimental import pallas as pl
from jax.experimental.pallas import tpu as pltpu
from jax.sharding import Mesh, PartitionSpec as P


F32 = jnp.float32
BF16 = jnp.bfloat16
N = 256
H = 128
PACK = 272
NS_STEPS = 3
WIDE, THIN = N // 4, N // 8
VMEM_BYTES = 8 * 1024 * 1024


def split(a):
    hi = a.astype(BF16)
    lo = (a - hi.astype(F32)).astype(BF16)
    return hi, lo


def mm(a, b):
    dot = functools.partial(jnp.dot, preferred_element_type=F32)
    return dot(a[0], b[0]) + (dot(a[0], b[1]) + dot(a[1], b[0]))


def eye_mask(n):
    i = lax.broadcasted_iota(jnp.int32, (n, n), 0)
    j = lax.broadcasted_iota(jnp.int32, (n, n), 1)
    return i, j


def column(row, n):
    i, j = eye_mask(n)
    return jnp.sum(jnp.where(i == j, row, 0.0), axis=1, keepdims=True)


def pack(m, out):
    i, j = eye_mask(H)
    first, corner = m[:H, :H], m[H:, H:]
    rows = jnp.where(i <= j, first, corner)
    diag = jnp.sum(jnp.where(i == j, corner, 0.0), axis=0, keepdims=True)
    tail = jnp.where(lax.broadcasted_iota(jnp.int32, (PACK - N, H), 0) == 0, diag, 0.0)
    out[:H, :] = rows
    out[H:N, :] = m[:H, H:]
    out[N:, :] = tail


def unpack(p):
    i, j = eye_mask(H)
    rows, cross, diag = p[:H], p[H:N], p[N:N + 1]
    turned = rows.T
    first = jnp.where(i <= j, rows, turned)
    corner = jnp.where(i > j, rows, jnp.where(i < j, turned, diag))
    top = jnp.concatenate([first, cross], axis=1)
    low = jnp.concatenate([cross.T, corner], axis=1)
    return jnp.concatenate([top, low], axis=0)


def gram_kernel(*refs):
    sources, out_ref, held, sems = refs[:4], refs[4], refs[5:9], refs[9]
    copies = [
        pltpu.make_async_copy(source, target, sems.at[place])
        for place, (source, target) in enumerate(zip(sources, held))
    ]
    for copy in copies:
        copy.start()
    for copy in copies:
        copy.wait()
    cur_ref, mean_ref, rows_ref, prec_ref = held
    value = cur_ref[...] + column(mean_ref[...], N)
    state_row = lax.broadcasted_iota(jnp.int32, (N, H), 0)
    chosen = (state_row == rows_ref[...]).astype(F32).T.astype(BF16)
    dot = functools.partial(jnp.dot, preferred_element_type=F32)
    one = value.astype(BF16)
    rest = value - one.astype(F32)
    two = rest.astype(BF16)
    three = (rest - two.astype(F32)).astype(BF16)
    picked = dot(chosen, one) + (dot(chosen, two) + dot(chosen, three))
    predicted = jnp.tanh(picked)
    centred = predicted - jnp.mean(predicted, axis=1, keepdims=True)
    centred = centred * jnp.sqrt(column(prec_ref[...], H))
    gram = mm(split(centred.T), split(centred)) * (1.0 / (N - 1))
    pack(gram, out_ref)


def halve_kernel(both_ref, out_ref):
    rows = pl.ds(pl.multiple_of(lax.axis_index("core") * (PACK // 2), 8), PACK // 2)
    total = both_ref[0, rows, :] + both_ref[1, rows, :]
    for copy in range(4):
        out_ref[copy] = total


def root_kernel(halves_ref, out_ref, packed):
    total = jnp.concatenate([halves_ref[0], halves_ref[1]], axis=0)
    i, j = eye_mask(N)
    unit = jnp.where(i == j, 1.0, 0.0)
    system = unpack(total) + unit
    square = jnp.sum(jnp.sum(system * system, axis=0, keepdims=True), axis=1, keepdims=True)
    root = system * (1.0 / jnp.sqrt(square))
    factor = 1.5 * unit - 0.5 * root
    inverse = split(factor)
    root = split(mm(split(root), inverse))
    for step in range(1, NS_STEPS):
        factor = split(1.5 * unit - 0.5 * mm(inverse, root))
        if step + 1 < NS_STEPS:
            root = split(mm(root, factor))
        last = mm(factor, inverse)
        inverse = split(last)
    diag = jnp.where(i == j, last, 0.0)
    trace = jnp.sum(jnp.sum(diag, axis=0, keepdims=True), axis=1, keepdims=True)
    pack(last * (N / trace), packed)
    core = lax.axis_index("core")
    half = packed[pl.ds(pl.multiple_of(core * (PACK // 2), 8), PACK // 2), :]
    for copy in range(4):
        out_ref[copy] = half


def transforms(parts_ref):
    out = []
    for place in range(4):
        out.append(unpack(jnp.concatenate([parts_ref[0, place], parts_ref[1, place]], axis=0)))
    return out


def slices(total_ref, wide_ref, thin_ref):
    chip = lax.axis_index("x")
    core = lax.axis_index("core")
    wide_ref[...] = total_ref[pl.ds(pl.multiple_of(chip * WIDE, 8), WIDE), :]
    thin_ref[...] = total_ref[pl.ds(pl.multiple_of(core * H + chip * THIN, 8), THIN), :]


def quad_kernel(parts_ref, total_ref, wide_ref, thin_ref):
    one, two, three, four = [split(t) for t in transforms(parts_ref)]
    total_ref[...] = mm(split(mm(one, two)), split(mm(three, four)))
    slices(total_ref, wide_ref, thin_ref)


def quad_apply_kernel(parts_ref, cur_ref, out_ref):
    mine = lax.axis_index("zl")
    out_ref[...] = cur_ref[...]
    for place in range(4):

        @pl.when(place >= mine)
        def _():
            t = unpack(jnp.concatenate([parts_ref[0, place], parts_ref[1, place]], axis=0))
            out_ref[...] = mm(split(out_ref[...]), split(t))


def joined(ring_ref):
    after = ring_ref[0, :, :WIDE].reshape(N, N)
    before = ring_ref[1, :, :WIDE].reshape(N, N)
    across = [ring_ref[core, :, WIDE:].reshape(H, N) for core in range(2)]
    return after, jnp.concatenate(across, axis=0), before


def ring_kernel(ring_ref, mine_ref, total_ref, half_ref, one, two):
    quad = lax.axis_index("zh")
    mine = split(mine_ref[...])
    after, across, before = [split(m) for m in joined(ring_ref)]

    @pl.when(quad % 2 == 0)
    def _():
        one[...] = mm(mine, after)
        two[...] = mm(across, before)

    @pl.when(quad % 2 == 1)
    def _():
        one[...] = mm(before, mine)
        two[...] = mm(after, across)

    @pl.when(quad < 2)
    def _():
        total_ref[...] = mm(split(one[...]), split(two[...]))

    @pl.when(quad >= 2)
    def _():
        total_ref[...] = mm(split(two[...]), split(one[...]))

    core = lax.axis_index("core")
    half_ref[...] = total_ref[pl.ds(pl.multiple_of(core * H, 8), H), :]


def ring_apply_kernel(ring_ref, cur_ref, out_ref):
    quad = lax.axis_index("zh")
    out_ref[...] = cur_ref[...]
    for place, later in enumerate(joined(ring_ref)):

        @pl.when(quad + place < 3)
        def _():
            out_ref[...] = mm(split(out_ref[...]), split(later))


def row_apply_kernel(near_ref, cur_ref, out_ref):
    row = lax.axis_index("y")
    second = jnp.concatenate([near_ref[0, N:], near_ref[1, N:]], axis=0)

    @pl.when(row == 0)
    def _():
        later = mm(split(second), split(near_ref[1, :N]))
        first = mm(split(cur_ref[...]), split(near_ref[0, :N]))
        out_ref[...] = mm(split(first), split(later))

    @pl.when(row == 1)
    def _():
        first = mm(split(cur_ref[...]), split(near_ref[0, :N]))
        out_ref[...] = mm(split(first), split(second))

    @pl.when(row == 2)
    def _():
        out_ref[...] = mm(split(cur_ref[...]), split(near_ref[0, :N]))

    @pl.when(row == 3)
    def _():
        out_ref[...] = cur_ref[...]


VMEM = pl.BlockSpec(memory_space=pltpu.VMEM)


def call(kernel, outs, args, products, scratch=(), space=VMEM, limit=VMEM_BYTES):
    many = isinstance(outs, list)
    shapes = [jax.ShapeDtypeStruct(s, F32) for s in (outs if many else [outs])]
    moved = sum(a.size * 4 for a in args) + sum(s.size * 4 for s in shapes)
    return pl.pallas_call(
        kernel,
        out_shape=shapes if many else shapes[0],
        in_specs=[space] * len(args),
        out_specs=[VMEM] * len(shapes) if many else VMEM,
        scratch_shapes=list(scratch),
        compiler_params=pltpu.CompilerParams(vmem_limit_bytes=limit),
        cost_estimate=pl.CostEstimate(
            flops=products * 6 * N * N * N, bytes_accessed=moved, transcendentals=0
        ),
    )(*args)


RING = 16
NEAR = [
    (2 * z + core, 2 * ((z + step) % RING) + core)
    for core, step in enumerate((-4, 4))
    for z in range(RING)
]
ACROSS = [(z, (11 - z) if z % 8 < 4 else (19 - z)) for z in range(RING)]


def from_later(steps):
    return [
        (2 * row + core, 2 * (row - back) + core)
        for core, back in enumerate(steps)
        for row in range(back, 4)
    ]


ROW_ODD = from_later((1, 3))
ROW_EVEN = [(row, row - 2) for row in range(2, 4)]


def smoother(anomalies, mean_state, obs_rows, obs_precision):
    current = anomalies[0]
    sources = (current, mean_state, obs_rows, obs_precision)
    gram = call(
        gram_kernel,
        (PACK, H),
        [pltpu.with_memory_space_constraint(a, pltpu.HBM) for a in sources],
        1,
        [pltpu.VMEM(a.shape, a.dtype) for a in sources] + [pltpu.SemaphoreType.DMA((4,))],
        pl.BlockSpec(memory_space=pltpu.HBM),
    )
    both = lax.all_gather(gram, "core")
    spread = call(halve_kernel, (4, PACK // 2, H), (both,), 0)
    parts = lax.all_to_all(spread, "x", 0, 0)
    parts = lax.all_gather((parts[0] + parts[1]) + (parts[2] + parts[3]), "core")
    half = call(root_kernel, (4, PACK // 2, H), (parts,), 6, [pltpu.VMEM((PACK, H), F32)])
    parts = lax.all_gather(lax.all_to_all(half, "zl", 0, 0), "core")
    full = (N, N)
    wide, thin = (WIDE, N), (THIN, N)
    total, wide, thin = call(quad_kernel, [full, wide, thin], (parts,), 3)
    current = call(quad_apply_kernel, full, (parts, current), 4)
    near = lax.ppermute(wide, ("zh", "zl", "core"), NEAR)
    across = lax.ppermute(thin, ("zh", "zl"), ACROSS)
    piece = jnp.concatenate([near, across], axis=0)
    piece = jnp.broadcast_to(piece, (4, WIDE + THIN, N))
    ring = lax.all_gather(lax.all_to_all(piece, "x", 0, 0), "core")
    square = pltpu.VMEM(full, F32)
    total, half = call(ring_kernel, [full, (H, N)], (ring, total), 3, [square, square])
    current = call(ring_apply_kernel, full, (ring, current), 3)
    near = lax.ppermute(total, ("y", "core"), ROW_ODD)
    across = lax.ppermute(half, "y", ROW_EVEN)
    near = lax.all_gather(jnp.concatenate([near, across], axis=0), "core")
    return call(row_apply_kernel, full, (near, current), 3)[None]


def solution(mesh):
    devices = mesh.devices.reshape(4, 4, 4, 4, 2)
    grid = Mesh(devices, ("y", "zh", "zl", "x", "core"))
    win, state = ("y", "zh", "zl"), ("x", "core")
    placed = (P(win, state, None), P(win, state), P(win, state), P(win, state))
    return jax.shard_map(
        smoother, mesh=grid, in_specs=placed, out_specs=P(win, state, None), check_vma=False
    )
```

```python
import functools

import jax
import jax.numpy as jnp
from jax import lax
from jax.experimental import pallas as pl
from jax.experimental.pallas import tpu as pltpu
from jax.sharding import Mesh, PartitionSpec as P


F32 = jnp.float32
BF16 = jnp.bfloat16
N = 256
H = 128
PACK = 272
NS_STEPS = 3
WIDE, THIN = N // 4, N // 8
VMEM_BYTES = 8 * 1024 * 1024


def split(a):
    hi = a.astype(BF16)
    lo = (a - hi.astype(F32)).astype(BF16)
    return hi, lo


def mm(a, b):
    dot = functools.partial(jnp.dot, preferred_element_type=F32)
    return dot(a[0], b[0]) + (dot(a[0], b[1]) + dot(a[1], b[0]))


def eye_mask(n):
    i = lax.broadcasted_iota(jnp.int32, (n, n), 0)
    j = lax.broadcasted_iota(jnp.int32, (n, n), 1)
    return i, j


def column(row, n):
    i, j = eye_mask(n)
    return jnp.sum(jnp.where(i == j, row, 0.0), axis=1, keepdims=True)


def pack(m, out):
    i, j = eye_mask(H)
    first, corner = m[:H, :H], m[H:, H:]
    rows = jnp.where(i <= j, first, corner)
    diag = jnp.sum(jnp.where(i == j, corner, 0.0), axis=0, keepdims=True)
    tail = jnp.where(lax.broadcasted_iota(jnp.int32, (PACK - N, H), 0) == 0, diag, 0.0)
    out[:H, :] = rows
    out[H:N, :] = m[:H, H:]
    out[N:, :] = tail


def unpack(p):
    i, j = eye_mask(H)
    rows, cross, diag = p[:H], p[H:N], p[N:N + 1]
    turned = rows.T
    first = jnp.where(i <= j, rows, turned)
    corner = jnp.where(i > j, rows, jnp.where(i < j, turned, diag))
    top = jnp.concatenate([first, cross], axis=1)
    low = jnp.concatenate([cross.T, corner], axis=1)
    return jnp.concatenate([top, low], axis=0)


def gram_kernel(*refs):
    sources, out_ref, held, sems = refs[:4], refs[4], refs[5:9], refs[9]
    copies = [
        pltpu.make_async_copy(source, target, sems.at[place])
        for place, (source, target) in enumerate(zip(sources, held))
    ]
    for copy in copies:
        copy.start()
    for copy in copies:
        copy.wait()
    cur_ref, mean_ref, rows_ref, prec_ref = held
    value = cur_ref[...] + column(mean_ref[...], N)
    state_row = lax.broadcasted_iota(jnp.int32, (N, H), 0)
    chosen = (state_row == rows_ref[...]).astype(F32).T.astype(BF16)
    dot = functools.partial(jnp.dot, preferred_element_type=F32)
    one = value.astype(BF16)
    rest = value - one.astype(F32)
    two = rest.astype(BF16)
    three = (rest - two.astype(F32)).astype(BF16)
    picked = dot(chosen, one) + (dot(chosen, two) + dot(chosen, three))
    predicted = jnp.tanh(picked)
    centred = predicted - jnp.mean(predicted, axis=1, keepdims=True)
    centred = centred * jnp.sqrt(column(prec_ref[...], H))
    gram = mm(split(centred.T), split(centred)) * (1.0 / (N - 1))
    pack(gram, out_ref)


def halve_kernel(both_ref, out_ref):
    rows = pl.ds(pl.multiple_of(lax.axis_index("core") * (PACK // 2), 8), PACK // 2)
    total = both_ref[0, rows, :] + both_ref[1, rows, :]
    for copy in range(4):
        out_ref[copy] = total


def root_kernel(halves_ref, out_ref, packed):
    total = jnp.concatenate([halves_ref[0], halves_ref[1]], axis=0)
    i, j = eye_mask(N)
    unit = jnp.where(i == j, 1.0, 0.0)
    system = unpack(total) + unit
    square = jnp.sum(jnp.sum(system * system, axis=0, keepdims=True), axis=1, keepdims=True)
    root = system * (1.0 / jnp.sqrt(square))
    factor = 1.5 * unit - 0.5 * root
    inverse = split(factor)
    root = split(mm(split(root), inverse))
    for step in range(1, NS_STEPS):
        factor = split(1.5 * unit - 0.5 * mm(inverse, root))
        if step + 1 < NS_STEPS:
            root = split(mm(root, factor))
        last = mm(factor, inverse)
        inverse = split(last)
    diag = jnp.where(i == j, last, 0.0)
    trace = jnp.sum(jnp.sum(diag, axis=0, keepdims=True), axis=1, keepdims=True)
    pack(last * (N / trace), packed)
    core = lax.axis_index("core")
    half = packed[pl.ds(pl.multiple_of(core * (PACK // 2), 8), PACK // 2), :]
    for copy in range(4):
        out_ref[copy] = half


def transforms(parts_ref):
    out = []
    for place in range(4):
        out.append(unpack(jnp.concatenate([parts_ref[0, place], parts_ref[1, place]], axis=0)))
    return out


def slices(total_ref, wide_ref, thin_ref):
    chip = lax.axis_index("x")
    core = lax.axis_index("core")
    wide_ref[...] = total_ref[pl.ds(pl.multiple_of(chip * WIDE, 8), WIDE), :]
    thin_ref[...] = total_ref[pl.ds(pl.multiple_of(core * H + chip * THIN, 8), THIN), :]


def quad_kernel(parts_ref, total_ref, wide_ref, thin_ref):
    one, two, three, four = [split(t) for t in transforms(parts_ref)]
    total_ref[...] = mm(split(mm(one, two)), split(mm(three, four)))
    slices(total_ref, wide_ref, thin_ref)


def quad_apply_kernel(parts_ref, cur_ref, out_ref):
    mine = lax.axis_index("zl")
    out_ref[...] = cur_ref[...]
    for place in range(4):

        @pl.when(place >= mine)
        def _():
            t = unpack(jnp.concatenate([parts_ref[0, place], parts_ref[1, place]], axis=0))
            out_ref[...] = mm(split(out_ref[...]), split(t))


def joined(ring_ref):
    across = ring_ref[0, :, :WIDE].reshape(N, N)
    after = ring_ref[1, :, :WIDE].reshape(N, N)
    before = [ring_ref[core, :, WIDE:].reshape(H, N) for core in range(2)]
    return after, across, jnp.concatenate(before, axis=0)


def ring_kernel(ring_ref, mine_ref, total_ref, half_ref, one, two):
    quad = lax.axis_index("zh")
    mine = split(mine_ref[...])
    after, across, before = [split(m) for m in joined(ring_ref)]

    @pl.when(quad % 2 == 0)
    def _():
        one[...] = mm(mine, after)
        two[...] = mm(across, before)

    @pl.when(quad % 2 == 1)
    def _():
        one[...] = mm(before, mine)
        two[...] = mm(after, across)

    @pl.when(quad < 2)
    def _():
        total_ref[...] = mm(split(one[...]), split(two[...]))

    @pl.when(quad >= 2)
    def _():
        total_ref[...] = mm(split(two[...]), split(one[...]))

    core = lax.axis_index("core")
    half_ref[...] = total_ref[pl.ds(pl.multiple_of(core * H, 8), H), :]


def ring_apply_kernel(ring_ref, cur_ref, out_ref):
    quad = lax.axis_index("zh")
    out_ref[...] = cur_ref[...]
    for place, later in enumerate(joined(ring_ref)):

        @pl.when(quad + place < 3)
        def _():
            out_ref[...] = mm(split(out_ref[...]), split(later))


def row_apply_kernel(near_ref, cur_ref, out_ref):
    row = lax.axis_index("y")
    second = jnp.concatenate([near_ref[0, N:], near_ref[1, N:]], axis=0)

    @pl.when(row == 0)
    def _():
        later = mm(split(second), split(near_ref[1, :N]))
        first = mm(split(cur_ref[...]), split(near_ref[0, :N]))
        out_ref[...] = mm(split(first), split(later))

    @pl.when(row == 1)
    def _():
        first = mm(split(cur_ref[...]), split(near_ref[0, :N]))
        out_ref[...] = mm(split(first), split(second))

    @pl.when(row == 2)
    def _():
        out_ref[...] = mm(split(cur_ref[...]), split(near_ref[0, :N]))

    @pl.when(row == 3)
    def _():
        out_ref[...] = cur_ref[...]


VMEM = pl.BlockSpec(memory_space=pltpu.VMEM)


def call(kernel, outs, args, products, scratch=(), space=VMEM, limit=VMEM_BYTES):
    many = isinstance(outs, list)
    shapes = [jax.ShapeDtypeStruct(s, F32) for s in (outs if many else [outs])]
    moved = sum(a.size * 4 for a in args) + sum(s.size * 4 for s in shapes)
    return pl.pallas_call(
        kernel,
        out_shape=shapes if many else shapes[0],
        in_specs=[space] * len(args),
        out_specs=[VMEM] * len(shapes) if many else VMEM,
        scratch_shapes=list(scratch),
        compiler_params=pltpu.CompilerParams(vmem_limit_bytes=limit),
        cost_estimate=pl.CostEstimate(
            flops=products * 6 * N * N * N, bytes_accessed=moved, transcendentals=0
        ),
    )(*args)


RING = 16
ACROSS = [(2 * z, 2 * ((11 - z) if z % 8 < 4 else (19 - z))) for z in range(RING)]
FIRST = ACROSS + [(2 * z + 1, 2 * ((z - 4) % RING) + 1) for z in range(RING)]
BEFORE = [(z, (z + 4) % RING) for z in range(RING)]


def from_later(steps):
    return [
        (2 * row + core, 2 * (row - back) + core)
        for core, back in enumerate(steps)
        for row in range(back, 4)
    ]


ROW_ODD = from_later((1, 3))
ROW_EVEN = [(row, row - 2) for row in range(2, 4)]


def smoother(anomalies, mean_state, obs_rows, obs_precision):
    current = anomalies[0]
    sources = (current, mean_state, obs_rows, obs_precision)
    gram = call(
        gram_kernel,
        (PACK, H),
        [pltpu.with_memory_space_constraint(a, pltpu.HBM) for a in sources],
        1,
        [pltpu.VMEM(a.shape, a.dtype) for a in sources] + [pltpu.SemaphoreType.DMA((4,))],
        pl.BlockSpec(memory_space=pltpu.HBM),
    )
    both = lax.all_gather(gram, "core")
    spread = call(halve_kernel, (4, PACK // 2, H), (both,), 0)
    parts = lax.all_to_all(spread, "x", 0, 0)
    parts = lax.all_gather((parts[0] + parts[1]) + (parts[2] + parts[3]), "core")
    half = call(root_kernel, (4, PACK // 2, H), (parts,), 6, [pltpu.VMEM((PACK, H), F32)])
    parts = lax.all_gather(lax.all_to_all(half, "zl", 0, 0), "core")
    full = (N, N)
    wide, thin = (WIDE, N), (THIN, N)
    total, wide, thin = call(quad_kernel, [full, wide, thin], (parts,), 3)
    current = call(quad_apply_kernel, full, (parts, current), 4)
    first = lax.ppermute(wide, ("zh", "zl", "core"), FIRST)
    before = lax.ppermute(thin, ("zh", "zl"), BEFORE)
    piece = jnp.concatenate([first, before], axis=0)
    piece = jnp.broadcast_to(piece, (4, WIDE + THIN, N))
    ring = lax.all_gather(lax.all_to_all(piece, "x", 0, 0), "core")
    square = pltpu.VMEM(full, F32)
    total, half = call(ring_kernel, [full, (H, N)], (ring, total), 3, [square, square])
    current = call(ring_apply_kernel, full, (ring, current), 3)
    near = lax.ppermute(total, ("y", "core"), ROW_ODD)
    across = lax.ppermute(half, "y", ROW_EVEN)
    near = lax.all_gather(jnp.concatenate([near, across], axis=0), "core")
    return call(row_apply_kernel, full, (near, current), 3)[None]


def solution(mesh):
    devices = mesh.devices.reshape(4, 4, 4, 4, 2)
    grid = Mesh(devices, ("y", "zh", "zl", "x", "core"))
    win, state = ("y", "zh", "zl"), ("x", "core")
    placed = (P(win, state, None), P(win, state), P(win, state), P(win, state))
    return jax.shard_map(
        smoother, mesh=grid, in_specs=placed, out_specs=P(win, state, None), check_vma=False
    )
```

```python
import functools

import jax
import jax.numpy as jnp
from jax import lax
from jax.experimental import pallas as pl
from jax.experimental.pallas import tpu as pltpu
from jax.sharding import Mesh, PartitionSpec as P


F32 = jnp.float32
BF16 = jnp.bfloat16
N = 256
H = 128
PACK = 272
NS_STEPS = 3
WIDE, THIN = N // 4, N // 8
VMEM_BYTES = 8 * 1024 * 1024


def split(a):
    hi = a.astype(BF16)
    lo = (a - hi.astype(F32)).astype(BF16)
    return hi, lo


def mm(a, b):
    dot = functools.partial(jnp.dot, preferred_element_type=F32)
    return dot(a[0], b[0]) + (dot(a[0], b[1]) + dot(a[1], b[0]))


def eye_mask(n):
    i = lax.broadcasted_iota(jnp.int32, (n, n), 0)
    j = lax.broadcasted_iota(jnp.int32, (n, n), 1)
    return i, j


def column(row, n):
    i, j = eye_mask(n)
    return jnp.sum(jnp.where(i == j, row, 0.0), axis=1, keepdims=True)


def pack(m, out):
    i, j = eye_mask(H)
    first, corner = m[:H, :H], m[H:, H:]
    rows = jnp.where(i <= j, first, corner)
    diag = jnp.sum(jnp.where(i == j, corner, 0.0), axis=0, keepdims=True)
    tail = jnp.where(lax.broadcasted_iota(jnp.int32, (PACK - N, H), 0) == 0, diag, 0.0)
    out[:H, :] = rows
    out[H:N, :] = m[:H, H:]
    out[N:, :] = tail


def unpack(p):
    i, j = eye_mask(H)
    rows, cross, diag = p[:H], p[H:N], p[N:N + 1]
    turned = rows.T
    first = jnp.where(i <= j, rows, turned)
    corner = jnp.where(i > j, rows, jnp.where(i < j, turned, diag))
    top = jnp.concatenate([first, cross], axis=1)
    low = jnp.concatenate([cross.T, corner], axis=1)
    return jnp.concatenate([top, low], axis=0)


def gram_kernel(*refs):
    sources, out_ref, held, sems = refs[:4], refs[4], refs[5:9], refs[9]
    copies = [
        pltpu.make_async_copy(source, target, sems.at[place])
        for place, (source, target) in enumerate(zip(sources, held))
    ]
    for copy in copies:
        copy.start()
    cur_ref, mean_ref, rows_ref, prec_ref = held
    for copy in copies[1:]:
        copy.wait()
    mean = column(mean_ref[...], N)
    weight = jnp.sqrt(column(prec_ref[...], H))
    state_row = lax.broadcasted_iota(jnp.int32, (N, H), 0)
    chosen = (state_row == rows_ref[...]).astype(F32).T.astype(BF16)
    copies[0].wait()
    value = cur_ref[...] + mean
    dot = functools.partial(jnp.dot, preferred_element_type=F32)
    one = value.astype(BF16)
    rest = value - one.astype(F32)
    two = rest.astype(BF16)
    three = (rest - two.astype(F32)).astype(BF16)
    picked = dot(chosen, one) + (dot(chosen, two) + dot(chosen, three))
    predicted = jnp.tanh(picked)
    centred = predicted - jnp.mean(predicted, axis=1, keepdims=True)
    centred = centred * weight
    gram = mm(split(centred.T), split(centred)) * (1.0 / (N - 1))
    pack(gram, out_ref)


def halve_kernel(both_ref, out_ref):
    rows = pl.ds(pl.multiple_of(lax.axis_index("core") * (PACK // 2), 8), PACK // 2)
    total = both_ref[0, rows, :] + both_ref[1, rows, :]
    for copy in range(4):
        out_ref[copy] = total


def root_kernel(halves_ref, out_ref, packed):
    total = jnp.concatenate([halves_ref[0], halves_ref[1]], axis=0)
    i, j = eye_mask(N)
    unit = jnp.where(i == j, 1.0, 0.0)
    system = unpack(total) + unit
    square = jnp.sum(jnp.sum(system * system, axis=0, keepdims=True), axis=1, keepdims=True)
    root = system * (1.0 / jnp.sqrt(square))
    factor = 1.5 * unit - 0.5 * root
    inverse = split(factor)
    root = split(mm(split(root), inverse))
    for step in range(1, NS_STEPS):
        factor = split(1.5 * unit - 0.5 * mm(inverse, root))
        if step + 1 < NS_STEPS:
            root = split(mm(root, factor))
        last = mm(factor, inverse)
        inverse = split(last)
    diag = jnp.where(i == j, last, 0.0)
    trace = jnp.sum(jnp.sum(diag, axis=0, keepdims=True), axis=1, keepdims=True)
    pack(last * (N / trace), packed)
    core = lax.axis_index("core")
    half = packed[pl.ds(pl.multiple_of(core * (PACK // 2), 8), PACK // 2), :]
    for copy in range(4):
        out_ref[copy] = half


def transforms(parts_ref):
    out = []
    for place in range(4):
        out.append(unpack(jnp.concatenate([parts_ref[0, place], parts_ref[1, place]], axis=0)))
    return out


def slices(total_ref, wide_ref, thin_ref):
    chip = lax.axis_index("x")
    core = lax.axis_index("core")
    wide_ref[...] = total_ref[pl.ds(pl.multiple_of(chip * WIDE, 8), WIDE), :]
    thin_ref[...] = total_ref[pl.ds(pl.multiple_of(core * H + chip * THIN, 8), THIN), :]


def quad_kernel(parts_ref, total_ref, wide_ref, thin_ref):
    one, two, three, four = [split(t) for t in transforms(parts_ref)]
    total_ref[...] = mm(split(mm(one, two)), split(mm(three, four)))
    slices(total_ref, wide_ref, thin_ref)


def quad_apply_kernel(parts_ref, cur_ref, out_ref):
    mine = lax.axis_index("zl")
    out_ref[...] = cur_ref[...]
    for place in range(4):

        @pl.when(place >= mine)
        def _():
            t = unpack(jnp.concatenate([parts_ref[0, place], parts_ref[1, place]], axis=0))
            out_ref[...] = mm(split(out_ref[...]), split(t))


def joined(ring_ref):
    after = ring_ref[0, :, :WIDE].reshape(N, N)
    before = ring_ref[1, :, :WIDE].reshape(N, N)
    across = [ring_ref[core, :, WIDE:].reshape(H, N) for core in range(2)]
    return after, jnp.concatenate(across, axis=0), before


def ring_kernel(ring_ref, mine_ref, total_ref, half_ref, one, two):
    quad = lax.axis_index("zh")
    mine = split(mine_ref[...])
    after, across, before = [split(m) for m in joined(ring_ref)]

    @pl.when(quad % 2 == 0)
    def _():
        one[...] = mm(mine, after)
        two[...] = mm(across, before)

    @pl.when(quad % 2 == 1)
    def _():
        one[...] = mm(before, mine)
        two[...] = mm(after, across)

    @pl.when(quad < 2)
    def _():
        total_ref[...] = mm(split(one[...]), split(two[...]))

    @pl.when(quad >= 2)
    def _():
        total_ref[...] = mm(split(two[...]), split(one[...]))

    core = lax.axis_index("core")
    half_ref[...] = total_ref[pl.ds(pl.multiple_of(core * H, 8), H), :]


def ring_apply_kernel(ring_ref, cur_ref, out_ref):
    quad = lax.axis_index("zh")
    out_ref[...] = cur_ref[...]
    for place, later in enumerate(joined(ring_ref)):

        @pl.when(quad + place < 3)
        def _():
            out_ref[...] = mm(split(out_ref[...]), split(later))


def row_apply_kernel(near_ref, cur_ref, out_ref):
    row = lax.axis_index("y")
    second = jnp.concatenate([near_ref[0, N:], near_ref[1, N:]], axis=0)

    @pl.when(row == 0)
    def _():
        later = mm(split(second), split(near_ref[1, :N]))
        first = mm(split(cur_ref[...]), split(near_ref[0, :N]))
        out_ref[...] = mm(split(first), split(later))

    @pl.when(row == 1)
    def _():
        first = mm(split(cur_ref[...]), split(near_ref[0, :N]))
        out_ref[...] = mm(split(first), split(second))

    @pl.when(row == 2)
    def _():
        out_ref[...] = mm(split(cur_ref[...]), split(near_ref[0, :N]))

    @pl.when(row == 3)
    def _():
        out_ref[...] = cur_ref[...]


VMEM = pl.BlockSpec(memory_space=pltpu.VMEM)


def call(kernel, outs, args, products, scratch=(), space=VMEM, limit=VMEM_BYTES):
    many = isinstance(outs, list)
    shapes = [jax.ShapeDtypeStruct(s, F32) for s in (outs if many else [outs])]
    moved = sum(a.size * 4 for a in args) + sum(s.size * 4 for s in shapes)
    return pl.pallas_call(
        kernel,
        out_shape=shapes if many else shapes[0],
        in_specs=[space] * len(args),
        out_specs=[VMEM] * len(shapes) if many else VMEM,
        scratch_shapes=list(scratch),
        compiler_params=pltpu.CompilerParams(vmem_limit_bytes=limit),
        cost_estimate=pl.CostEstimate(
            flops=products * 6 * N * N * N, bytes_accessed=moved, transcendentals=0
        ),
    )(*args)


RING = 16
NEAR = [
    (2 * z + core, 2 * ((z + step) % RING) + core)
    for core, step in enumerate((-4, 4))
    for z in range(RING)
]
ACROSS = [(z, (11 - z) if z % 8 < 4 else (19 - z)) for z in range(RING)]


def from_later(steps):
    return [
        (2 * row + core, 2 * (row - back) + core)
        for core, back in enumerate(steps)
        for row in range(back, 4)
    ]


ROW_ODD = from_later((1, 3))
ROW_EVEN = [(row, row - 2) for row in range(2, 4)]


def smoother(anomalies, mean_state, obs_rows, obs_precision):
    current = anomalies[0]
    sources = (current, mean_state, obs_rows, obs_precision)
    gram = call(
        gram_kernel,
        (PACK, H),
        [pltpu.with_memory_space_constraint(a, pltpu.HBM) for a in sources],
        1,
        [pltpu.VMEM(a.shape, a.dtype) for a in sources] + [pltpu.SemaphoreType.DMA((4,))],
        pl.BlockSpec(memory_space=pltpu.HBM),
    )
    both = lax.all_gather(gram, "core")
    spread = call(halve_kernel, (4, PACK // 2, H), (both,), 0)
    parts = lax.all_to_all(spread, "x", 0, 0)
    parts = lax.all_gather((parts[0] + parts[1]) + (parts[2] + parts[3]), "core")
    half = call(root_kernel, (4, PACK // 2, H), (parts,), 6, [pltpu.VMEM((PACK, H), F32)])
    parts = lax.all_gather(lax.all_to_all(half, "zl", 0, 0), "core")
    full = (N, N)
    wide, thin = (WIDE, N), (THIN, N)
    total, wide, thin = call(quad_kernel, [full, wide, thin], (parts,), 3)
    current = call(quad_apply_kernel, full, (parts, current), 4)
    near = lax.ppermute(wide, ("zh", "zl", "core"), NEAR)
    across = lax.ppermute(thin, ("zh", "zl"), ACROSS)
    piece = jnp.concatenate([near, across], axis=0)
    piece = jnp.broadcast_to(piece, (4, WIDE + THIN, N))
    ring = lax.all_gather(lax.all_to_all(piece, "x", 0, 0), "core")
    square = pltpu.VMEM(full, F32)
    total, half = call(ring_kernel, [full, (H, N)], (ring, total), 3, [square, square])
    current = call(ring_apply_kernel, full, (ring, current), 3)
    near = lax.ppermute(total, ("y", "core"), ROW_ODD)
    across = lax.ppermute(half, "y", ROW_EVEN)
    near = lax.all_gather(jnp.concatenate([near, across], axis=0), "core")
    return call(row_apply_kernel, full, (near, current), 3)[None]


def solution(mesh):
    devices = mesh.devices.reshape(4, 4, 4, 4, 2)
    grid = Mesh(devices, ("y", "zh", "zl", "x", "core"))
    win, state = ("y", "zh", "zl"), ("x", "core")
    placed = (P(win, state, None), P(win, state), P(win, state), P(win, state))
    return jax.shard_map(
        smoother, mesh=grid, in_specs=placed, out_specs=P(win, state, None), check_vma=False
    )
```
